32 devices in a mesh: row: 4 (over x, core), col: 8 (over z, y).
Axes of the slice: x: 2, y: 2, z: 4, core: 2. Of those that a mesh axis runs over, the one named last changes fastest.
Arguments:
- adjacency_tiles: bfloat16 [4, 8, 80, 128, 128], P('row', 'col'), may hold values from -0.09375 to 0.09375
- tile_rows: int32 [4, 8, 80], P('row', 'col'), may hold values from 0 to 15, as said below
- tile_cols: int32 [4, 8, 80], P('row', 'col'), may hold values from 0 to 7, as said below
- tile_counts: int32 [4, 8], P('row', 'col'), may hold values from 40 to 80, as said below
- features: bfloat16 [8192, 1024], P('col', 'row'), may hold values from -6 to 6
- weight: bfloat16 [1024, 1024], P('col'), may hold values from -0.1875 to 0.1875
Outputs:
- activated: bfloat16 [8192, 1024], P(('row', 'col'))
The draws below stay inside these ranges and needn't reach their ends.
Inputs may be any that keep to these rules, and one draw needn't show every extreme that they name: `tile_counts`: some grid cell holds exactly 80 live tiles in every draw. In each grid cell the first tile_counts entries of tile_rows and tile_cols name distinct (row, column) tile pairs; later entries are valid indices but unused. `tile_cols`: see tile_rows.
All inputs are finite; a program needn't handle non-finite values.
Results may differ from the reference program's by a relative error of at most 0.014.
Values may be sent and summed in bfloat16 or wider, within the bound.
A program may use at most 64 MiB of HBM per device.

```python
import jax
import jax.numpy as jnp
from jax import lax

F = 1024
TB = 128
CB_DEV = 8
CAP = 80
RB_DEV = 16
NODES = 8192
N_ROW = 4
N_COL = 8


def layout_draw(key):
    base = jax.random.fold_in(key, 7)
    key_first, key_busy, key_slots = jax.random.split(base, 3)
    cells = N_ROW * N_COL
    lowest = CAP // 2
    counts = jax.random.randint(key_first, (N_ROW, N_COL), lowest, CAP + 1)
    busiest = jax.random.randint(key_busy, (), 0, cells)
    flat_index = jnp.arange(cells).reshape(N_ROW, N_COL)
    counts = jnp.where(flat_index == busiest, CAP, counts)
    slot_keys = jax.random.split(key_slots, cells)
    orders = jax.vmap(lambda single: jax.random.permutation(single, RB_DEV * CB_DEV)[:CAP])(slot_keys)
    orders = orders.reshape(N_ROW, N_COL, CAP)
    return (counts.astype(jnp.int32), (orders // CB_DEV).astype(jnp.int32), (orders % CB_DEV).astype(jnp.int32))


def draw_tile_rows(key, part):
    return layout_draw(key)[1]


def draw_tile_cols(key, part):
    return layout_draw(key)[2]


def draw_tile_counts(key, part):
    return layout_draw(key)[0]


def level_of(key, shape, cuts, smallest, high):
    def one(position, shards_of):
        draws = jax.random.uniform(jax.random.fold_in(jax.random.fold_in(key, 6), position), (shards_of,), jnp.float32, smallest / len(cuts), high / len(cuts))
        return jnp.repeat(jnp.exp(draws), shape[position] // shards_of).reshape((-1,) + (1,) * (len(shape) - position - 1))

    gain = one(*cuts[0])
    for cut in cuts[1:]:
        gain = gain * one(*cut)
    return gain


def scatter_about(key, dims, scale, limit, shards=(), kind=jnp.bfloat16):
    array = scale * jax.random.normal(key, dims, jnp.float32)
    if shards:
        array = array * level_of(key, dims, shards, -0.22, 0.18)
    return jnp.clip(array, -limit, limit).astype(kind)


def setup_inputs(seed: int = 0) -> dict:
    streams_of = jax.random.split(jax.random.key(seed), 7)
    adjacency_tiles = scatter_about(streams_of[0], (N_ROW, N_COL, CAP, TB, TB), (TB * CAP * N_COL * 3 // (4 * RB_DEV)) ** -0.5, 0.09375, ((0, 4), (1, 8)))
    tile_rows = draw_tile_rows(jax.random.fold_in(streams_of[6], 71), 0)
    tile_cols = draw_tile_cols(jax.random.fold_in(streams_of[6], 71), 0)
    tile_counts = draw_tile_counts(jax.random.fold_in(streams_of[6], 71), 0)
    features = scatter_about(streams_of[4], (NODES, F), 1.0, 6.0, ((0, 8), (1, 4)))
    weight = scatter_about(streams_of[5], (F, F), F ** -0.5, 0.1875, ((0, 8),))
    return dict(adjacency_tiles=adjacency_tiles, tile_rows=tile_rows, tile_cols=tile_cols, tile_counts=tile_counts, features=features, weight=weight)


def accumulate(adjacency_tiles, tile_rows, tile_cols, tile_count, feature_blocks, row_blocks):
    tile_edge = adjacency_tiles.shape[1]
    panel_width = feature_blocks.shape[2]
    group_count = (tile_count + 7) // 8

    def add_group(group_index, totals):
        for member in range(8):
            slot_index = group_index * 8 + member
            one_tile = lax.dynamic_index_in_dim(adjacency_tiles, slot_index, 0, keepdims=False)
            row_block = tile_rows[slot_index]
            col_block = tile_cols[slot_index]
            source = lax.dynamic_index_in_dim(feature_blocks, col_block, 0, keepdims=False)
            product = jnp.dot(one_tile, source, preferred_element_type=jnp.float32)
            is_live = (slot_index < tile_count).astype(jnp.float32)
            current = lax.dynamic_index_in_dim(totals, row_block, 0, keepdims=True)
            totals = lax.dynamic_update_index_in_dim(totals, current + is_live * product[None], row_block, 0)
        return totals

    start_totals = jnp.zeros((row_blocks, tile_edge, panel_width), jnp.float32)
    return lax.fori_loop(jnp.int32(0), group_count.astype(jnp.int32), add_group, start_totals)


def reference(adjacency_tiles, tile_rows, tile_cols, tile_counts, features, weight):
    feature_all = features.reshape(N_COL, CB_DEV, TB, F)

    def row_stripe(row_index):
        def add_column(running, col_index):
            partial_value = accumulate(adjacency_tiles[row_index, col_index], tile_rows[row_index, col_index],
                                 tile_cols[row_index, col_index], tile_counts[row_index, col_index],
                                 feature_all[col_index], RB_DEV)
            rounded = lax.optimization_barrier(partial_value.astype(jnp.bfloat16))
            return running + rounded.astype(jnp.float32), None

        running, unused = lax.scan(add_column, jnp.zeros((RB_DEV, TB, F), jnp.float32),
                                   jnp.arange(N_COL, dtype=jnp.int32))
        return running.reshape(RB_DEV * TB, F)

    aggregated = lax.map(row_stripe, jnp.arange(N_ROW, dtype=jnp.int32)).reshape(NODES, F).astype(jnp.bfloat16)
    hidden = jnp.dot(aggregated, weight, preferred_element_type=jnp.float32)
    return jnp.maximum(hidden, 0.0).astype(jnp.bfloat16)
```

```python
import functools

import jax
import jax.numpy as jnp
from jax import lax
from jax.experimental import pallas as pl
from jax.experimental.pallas import tpu as pltpu
from jax.sharding import PartitionSpec as P

MESH = pl.DeviceIdType.MESH


def densify(adjacency_tiles, tile_rows, tile_cols, tile_count, row_blocks, column_blocks):
    slots = adjacency_tiles.shape[0]
    tile_edge = adjacency_tiles.shape[1]
    live_mask = (jnp.arange(slots, dtype=jnp.int32) < tile_count).astype(jnp.bfloat16)
    masked = adjacency_tiles * live_mask[:, None, None]
    grid = jnp.zeros((row_blocks, column_blocks, tile_edge, tile_edge), jnp.bfloat16)
    grid = grid.at[tile_rows, tile_cols].add(masked)
    return grid.transpose(0, 2, 1, 3).reshape(row_blocks * tile_edge, column_blocks * tile_edge)


def reduce_whole(partial_rows):
    return lax.psum_scatter(
        partial_rows.astype(jnp.bfloat16), "col", scatter_dimension=0, tiled=True
    ).astype(jnp.float32)


def shards(adjacency_tiles, tile_rows, tile_cols, tile_counts, features, weight):
    local_tiles = adjacency_tiles[0, 0]
    local_rows = tile_rows[0, 0]
    local_cols = tile_cols[0, 0]
    local_count = tile_counts[0, 0]
    tile_edge = local_tiles.shape[1]
    column_blocks = features.shape[0] // tile_edge
    row_blocks = column_blocks * lax.axis_size("col") // lax.axis_size("row")
    dense_block = densify(
        local_tiles, local_rows, local_cols, local_count, row_blocks, column_blocks
    )
    whole = lax.all_gather(features, "row", axis=1, tiled=True)
    partial_value = jnp.dot(dense_block, whole, preferred_element_type=jnp.float32)
    summed = reduce_whole(partial_value.astype(jnp.bfloat16).astype(jnp.float32))
    aggregated = summed.astype(jnp.bfloat16)
    full_weight = lax.all_gather(weight, "col", axis=0, tiled=True)
    hidden = jnp.dot(aggregated, full_weight, preferred_element_type=jnp.float32)
    return jnp.maximum(hidden, 0.0).astype(jnp.bfloat16)


def layer_kernel(
    inv, adj_hbm, feat_hbm, w_hbm, out_ref,
    adj, dense, feat, wfull, psend, own, yr, zp, zm, zb, acc, hidden,
    lsem, fsend, frecv, wsend, wrecv, vsend, vrecv, ysend, yrecv, psem, prsem, msem, mrsem, bsend, brecv,
):
    p, q = lax.axis_index("row"), lax.axis_index("col")
    y, z = q % 2, q // 2
    mate = p + 1 - 2 * (p % 2)
    across = (p + 2) % 4
    half = z // 2
    pair_z = z + 1 - 2 * (z % 2)
    q_y, q_pair, q_mid = 2 * z + 1 - y, 2 * pair_z + y, 2 * (3 - z) + y
    is_end = z % 3 == 0
    is_mid = z % 3 > 0
    slots = adj_hbm.shape[0]
    tb = adj_hbm.shape[1]
    quarter = wfull.shape[2]

    def at(i):
        return i + half * (3 - 2 * i)

    barrier = pltpu.get_barrier_semaphore()
    for to in ({"col": q_y}, {"row": mate}, {"row": across}, {"col": q_pair}):
        pl.semaphore_signal(barrier, inc=1, device_id=to, device_id_type=MESH)

    @pl.when(is_mid)
    def _():
        pl.semaphore_signal(barrier, inc=1, device_id={"col": q_mid}, device_id_type=MESH)

    cp_adj = pltpu.make_async_copy(adj_hbm, adj.at[pl.ds(0, slots)], lsem.at[0])
    cp_adj.start()
    cp_feat = pltpu.make_async_copy(feat_hbm, feat.at[0], lsem.at[1])
    cp_feat.start()
    w_mine = w_hbm.at[pl.ds(pl.multiple_of(p * quarter, quarter), quarter)]
    cp_w = pltpu.make_async_copy(w_mine, wfull.at[q, p], lsem.at[2])
    cp_w.start()

    def copy_to(src, dst, ssem, rsem, **to):
        return pltpu.make_async_remote_copy(
            src_ref=src, dst_ref=dst, send_sem=ssem, recv_sem=rsem, device_id=to, device_id_type=MESH)

    f_mate = copy_to(feat_hbm, feat.at[1], fsend.at[0], frecv.at[0], row=mate)
    f_across = copy_to(feat_hbm, feat.at[2], fsend.at[1], frecv.at[1], row=across)
    f_fwd = copy_to(feat.at[2], feat.at[3], fsend.at[2], frecv.at[2], row=mate)
    v_mate = copy_to(wfull.at[:, p], wfull.at[:, p], vsend.at[0], vrecv.at[0], row=mate)
    v_across = copy_to(wfull.at[:, p], wfull.at[:, p], vsend.at[1], vrecv.at[1], row=across)
    v_fwd = copy_to(wfull.at[:, across], wfull.at[:, across], vsend.at[2], vrecv.at[2], row=mate)

    def w_copy(n, ref, to):
        return copy_to(ref, ref, wsend.at[n], wrecv.at[n], col=to)

    def w_block(at_q):
        return wfull.at[at_q, p]

    def w_blocks(first, count):
        return wfull.at[pl.ds(first, count), p]

    w_up = w_copy(0, w_block(q), q_pair)
    w_own_y = w_copy(1, w_block(q), q_y)
    w_end_y = w_copy(2, w_block(q_pair), q_y)
    w_mids = w_copy(3, w_blocks(2 * z, 2), q_pair)
    w_end = w_copy(4, w_block(2 * pair_z + 1 - y), q_pair)
    w_half = w_copy(5, w_blocks(4 * half, 4), q_mid)
    w_other = w_copy(6, w_blocks(4 - 4 * half, 4), q_pair)
    r_up = w_copy(0, w_block(q_pair), q_pair)
    r_own_y = w_copy(1, w_block(q_y), q_y)
    r_end_y = w_copy(2, w_block(2 * pair_z + 1 - y), q_y)
    r_mids = w_copy(3, w_blocks(2 * pair_z, 2), q_pair)
    r_end = w_copy(4, w_block(q_y), q_pair)
    r_half = w_copy(5, w_blocks(4 - 4 * half, 4), q_mid)
    r_other = w_copy(6, w_blocks(4 - 4 * half, 4), q_pair)

    def y_copy(k, i):
        d = at(i)
        return copy_to(psend.at[k, d], yr.at[k, d], ysend.at[k, d], yrecv.at[k, d], col=q_y)

    def p_copy(k, i):
        d = at(i)
        return copy_to(own.at[k, d], zp.at[k, d], psem.at[k, d], prsem.at[k, d], col=q_pair)

    def m_copy(k, i):
        d = at(i)
        return copy_to(own.at[k, d], zm.at[k, d], msem.at[k, d], mrsem.at[k, d], col=q_mid)

    def b_copy(k):
        return copy_to(psend.at[k, at(0)], zb.at[k], bsend.at[k], brecv.at[k], col=q_pair)

    def densify(side, d):
        base = (2 * d + side) * 16
        for up in range(2):
            for cb in range(8):
                dense[side, d, up * tb:(up + 1) * tb, cb * tb:(cb + 1) * tb] = adj[inv[base + up * 8 + cb]]

    def product(k, side, d):
        return jnp.dot(dense[side, d], feat[k], preferred_element_type=jnp.float32).astype(jnp.bfloat16)

    def total(refs):
        out = refs[0][...].astype(jnp.float32)
        for ref in refs[1:]:
            out = out + ref[...].astype(jnp.float32)
        return out.astype(jnp.bfloat16)

    def add_end(k, i):
        d = at(i)
        y_copy(k, i).wait_recv()
        own[k, d] = total([own.at[k, d], yr.at[k, d]])
        p_copy(k, i).start()

    def add_mid(k, i):
        d = at(i)
        y_copy(k, i).wait_recv()
        p_copy(k, i).wait_recv()
        own[k, d] = total([own.at[k, d], yr.at[k, d], zp.at[k, d]])
        m_copy(k, i).start()

    def add_out(k):
        d = at(0)
        m_copy(k, 0).wait_recv()
        if k < 2:
            y_copy(k, 0).wait_recv()
            own[k, d] = total([own.at[k, d], yr.at[k, d], zm.at[k, d]])
        else:
            own[k, d] = total([own.at[k, d], zm.at[k, d]])
        p_copy(k, 0).start()

    def merge(k):
        d = at(0)
        b_copy(k).wait_recv()
        psend[k, d] = total([psend.at[k, d], zb.at[k]])
        y_copy(k, 0).start()

    def settle(k):
        @pl.when(is_end)
        def _():
            p_copy(k, 0).wait_recv()
            if k < 2:
                acc[...] = total([own.at[k, z], zp.at[k, z]])
            else:
                y_copy(k, 0).wait_recv()
                acc[...] = total([own.at[k, z], zp.at[k, z], yr.at[k, z]])

        @pl.when(is_mid)
        def _():
            y_copy(k, 1).wait_recv()
            m_copy(k, 1).wait_recv()
            p_copy(k, 1).wait_recv()
            acc[...] = total([own.at[k, z], yr.at[k, z], zm.at[k, z], zp.at[k, z]])

    panels = (p, mate, across, (mate + 2) % 4)

    def finish(k):
        settle(k)
        rows = wfull[pl.ds(2 * panels[k], 2)].reshape(8 * quarter, wfull.shape[3])
        term = jnp.dot(acc[...], rows, preferred_element_type=jnp.float32)
        if k == 0:
            hidden[...] = term
        elif k < 3:
            hidden[...] += term
        else:
            out_ref[...] = jnp.maximum(hidden[...] + term, 0.0).astype(jnp.bfloat16)

    adj[slots] = jnp.zeros((tb, tb), jnp.bfloat16)
    cp_adj.wait()
    cp_feat.wait()
    densify(1 - y, at(3))
    psend[0, at(3)] = product(0, 1 - y, at(3))
    cp_w.wait()
    pl.semaphore_wait(barrier, 4 + (z + 1) % 4 // 2)

    y_copy(0, 3).start()
    f_mate.start()
    f_across.start()

    @pl.when(is_end)
    def _():
        w_up.start()

    @pl.when(is_mid)
    def _():
        w_own_y.start()

    @pl.loop(0, 3)
    def _(step):
        d = at(2 - step)
        densify(1 - y, d)
        psend[0, d] = product(0, 1 - y, d)

        @pl.when(step == 0)
        def _():
            y_copy(0, 2).start()

    @pl.when(is_end)
    def _():
        b_copy(0).start()

    f_mate.wait_recv()

    @pl.loop(0, 4)
    def _(step):
        d = at(3 - step)
        psend[1, d] = product(1, 1 - y, d)

        @pl.when(step < 2)
        def _():
            y_copy(1, 3 - step).start()

    y_copy(0, 1).start()

    @pl.when(is_end)
    def _():
        b_copy(1).start()
        y_copy(1, 1).start()

    @pl.loop(0, 4)
    def _(step):
        d = at(3 - step)
        densify(y, d)
        own[0, d] = product(0, y, d)
        own[1, d] = product(1, y, d)

    @pl.when(is_end)
    def _():
        add_end(0, 3)
        add_end(0, 2)
        add_end(1, 3)
        add_end(1, 2)

    @pl.when(is_mid)
    def _():
        r_up.wait_recv()
        w_end_y.start()
        merge(0)
        merge(1)
        y_copy(1, 1).start()
        r_own_y.wait_recv()
        w_mids.start()
        r_end_y.wait_recv()
        w_end.start()
        w_half.start()
        add_mid(0, 3)

    f_across.wait_recv()
    f_fwd.start()

    @pl.loop(0, 4)
    def _(step):
        d = at(3 - step)
        psend[2, d] = product(2, 1 - y, d)

        @pl.when(step == 0)
        def _():
            y_copy(2, 3).start()

    @pl.when(is_mid)
    def _():
        b_copy(2).start()
        add_mid(0, 2)

    f_fwd.wait_recv()

    @pl.loop(0, 4)
    def _(step):
        d = at(3 - step)
        psend[3, d] = product(3, 1 - y, d)

        @pl.when(step == 0)
        def _():
            y_copy(3, 3).start()
            y_copy(2, 2).start()

        @pl.when(step == 1)
        def _():
            y_copy(3, 2).start()
            y_copy(2, 1).start()

    y_copy(3, 1).start()

    @pl.when(is_mid)
    def _():
        b_copy(3).start()

    @pl.when(is_end)
    def _():
        add_end(0, 1)

    @pl.loop(0, 4)
    def _(step):
        d = at(3 - step)
        own[2, d] = product(2, y, d)
        own[3, d] = product(3, y, d)

    @pl.when(is_end)
    def _():
        add_end(1, 1)
        r_mids.wait_recv()
        r_end.wait_recv()
        r_other.wait_recv()
        v_across.start()
        v_mate.start()
        merge(2)
        merge(3)
        add_end(2, 3)
        add_end(3, 3)
        add_end(2, 2)
        add_end(3, 2)

    @pl.when(is_mid)
    def _():
        add_mid(1, 3)
        r_half.wait_recv()
        w_other.start()
        v_across.start()
        v_mate.start()
        add_out(0)
        add_mid(1, 2)
        add_out(1)
        add_mid(2, 3)
        add_mid(3, 3)

    v_across.wait_recv()
    v_fwd.start()

    @pl.when(is_end)
    def _():
        add_end(2, 1)

    @pl.when(is_mid)
    def _():
        add_out(2)
        add_mid(2, 2)

    v_mate.wait_recv()
    v_fwd.wait_recv()
    finish(0)
    finish(1)

    @pl.when(is_end)
    def _():
        add_end(3, 1)

    @pl.when(is_mid)
    def _():
        add_out(3)
        add_mid(3, 2)

    finish(2)
    finish(3)

    for copy in (f_mate, f_across, f_fwd, v_mate, v_across, v_fwd):
        copy.wait_send()

    @pl.loop(0, 4)
    def _(k):
        for i in (1, 2, 3):
            y_copy(k, i).wait_send()

    @pl.when(is_end)
    def _():
        w_up.wait_send()
        for k in (0, 1):
            b_copy(k).wait_send()
            y_copy(k + 2, 0).wait_send()

        @pl.loop(0, 4)
        def _(k):
            for i in (1, 2, 3):
                p_copy(k, i).wait_send()

    @pl.when(is_mid)
    def _():
        for copy in (w_own_y, w_end_y, w_mids, w_end, w_half, w_other):
            copy.wait_send()
        for k in (0, 1):
            b_copy(k + 2).wait_send()
            y_copy(k, 0).wait_send()

        @pl.loop(0, 4)
        def _(k):
            p_copy(k, 0).wait_send()
            m_copy(k, 3).wait_send()
            m_copy(k, 2).wait_send()


def fused_shards(adjacency_tiles, tile_rows, tile_cols, tile_counts, features, weight):
    tiles = adjacency_tiles[0, 0]
    slots, tb = tiles.shape[:2]
    live = jnp.arange(slots, dtype=jnp.int32)
    key = tile_rows[0, 0] * 8 + tile_cols[0, 0]
    place = jnp.arange(128, dtype=jnp.int32)
    hit = (place[:, None] == key[None, :]) & (live[None, :] < tile_counts[0, 0])
    inv = jnp.min(jnp.where(hit, live[None, :], slots), axis=1)
    width = features.shape[1]
    wide = weight.shape[1]
    bf = jnp.bfloat16
    dma = pltpu.SemaphoreType.DMA
    blocks = (4, 4, 256, width)
    return pl.pallas_call(
        layer_kernel,
        out_shape=jax.ShapeDtypeStruct((256, wide), bf),
        in_specs=[pl.BlockSpec(memory_space=pltpu.SMEM)]
        + [pl.BlockSpec(memory_space=pltpu.HBM)] * 3,
        out_specs=pl.BlockSpec(memory_space=pltpu.VMEM),
        scratch_shapes=[
            pltpu.VMEM((slots + 1, tb, tb), bf),
            pltpu.VMEM((2, 4, 256, 1024), bf),
            pltpu.VMEM((4, 1024, width), bf),
            pltpu.VMEM((8, 4, weight.shape[0] // 4, wide), bf),
            pltpu.VMEM(blocks, bf),
            pltpu.VMEM(blocks, bf),
            pltpu.VMEM(blocks, bf),
            pltpu.VMEM(blocks, bf),
            pltpu.VMEM(blocks, bf),
            pltpu.VMEM((4, 256, width), bf),
            pltpu.VMEM((256, width), bf),
            pltpu.VMEM((256, wide), jnp.float32),
            dma((3,)),
            dma((3,)), dma((3,)),
            dma((7,)), dma((7,)),
            dma((3,)), dma((3,)),
            dma((4, 4)), dma((4, 4)),
            dma((4, 4)), dma((4, 4)),
            dma((4, 4)), dma((4, 4)),
            dma((4,)), dma((4,)),
        ],
        compiler_params=pltpu.CompilerParams(
            collective_id=0, has_side_effects=True, vmem_limit_bytes=48 * 2**20),
    )(inv, *(pltpu.with_memory_space_constraint(a, pltpu.HBM) for a in (tiles, features, weight)))


def solution(mesh):
    fits = mesh.shape["row"] == 4 and mesh.shape["col"] == 8
    return jax.shard_map(
        fused_shards if fits else shards,
        mesh=mesh,
        in_specs=(
            P("row", "col", None, None, None),
            P("row", "col", None),
            P("row", "col", None),
            P("row", "col"),
            P("col", "row"),
            P("col", None),
        ),
        out_specs=P(("row", "col"), None),
        check_vma=False,
    )
```

```python
import functools

import jax
import jax.numpy as jnp
from jax import lax
from jax.experimental import pallas as pl
from jax.experimental.pallas import tpu as pltpu
from jax.sharding import PartitionSpec as P

MESH = pl.DeviceIdType.MESH


def densify(adjacency_tiles, tile_rows, tile_cols, tile_count, row_blocks, column_blocks):
    slots = adjacency_tiles.shape[0]
    tile_edge = adjacency_tiles.shape[1]
    live_mask = (jnp.arange(slots, dtype=jnp.int32) < tile_count).astype(jnp.bfloat16)
    masked = adjacency_tiles * live_mask[:, None, None]
    grid = jnp.zeros((row_blocks, column_blocks, tile_edge, tile_edge), jnp.bfloat16)
    grid = grid.at[tile_rows, tile_cols].add(masked)
    return grid.transpose(0, 2, 1, 3).reshape(row_blocks * tile_edge, column_blocks * tile_edge)


def reduce_whole(partial_rows):
    return lax.psum_scatter(
        partial_rows.astype(jnp.bfloat16), "col", scatter_dimension=0, tiled=True
    ).astype(jnp.float32)


def shards(adjacency_tiles, tile_rows, tile_cols, tile_counts, features, weight):
    local_tiles = adjacency_tiles[0, 0]
    local_rows = tile_rows[0, 0]
    local_cols = tile_cols[0, 0]
    local_count = tile_counts[0, 0]
    tile_edge = local_tiles.shape[1]
    column_blocks = features.shape[0] // tile_edge
    row_blocks = column_blocks * lax.axis_size("col") // lax.axis_size("row")
    dense_block = densify(
        local_tiles, local_rows, local_cols, local_count, row_blocks, column_blocks
    )
    whole = lax.all_gather(features, "row", axis=1, tiled=True)
    partial_value = jnp.dot(dense_block, whole, preferred_element_type=jnp.float32)
    summed = reduce_whole(partial_value.astype(jnp.bfloat16).astype(jnp.float32))
    aggregated = summed.astype(jnp.bfloat16)
    full_weight = lax.all_gather(weight, "col", axis=0, tiled=True)
    hidden = jnp.dot(aggregated, full_weight, preferred_element_type=jnp.float32)
    return jnp.maximum(hidden, 0.0).astype(jnp.bfloat16)


def layer_kernel(
    inv, adj_hbm, feat_hbm, w_hbm, out_ref,
    adj, dense, feat, wfull, psend, own, yr, zp, zm, zb, mb, acc, hidden,
    lsem, fsend, frecv, wsend, wrecv, vsend, vrecv, ysend, yrecv, psem, prsem, msem, mrsem, bsend, brecv, gsem,
):
    p, q = lax.axis_index("row"), lax.axis_index("col")
    y, z = q % 2, q // 2
    mate = p + 1 - 2 * (p % 2)
    across = (p + 2) % 4
    half = z // 2
    pair_z = z + 1 - 2 * (z % 2)
    q_y, q_pair, q_mid = 2 * z + 1 - y, 2 * pair_z + y, 2 * (3 - z) + y
    is_end = z % 3 == 0
    is_mid = z % 3 > 0
    slots = adj_hbm.shape[0]
    tb = adj_hbm.shape[1]
    quarter = wfull.shape[2]

    def at(i):
        return i + half * (3 - 2 * i)

    barrier = pltpu.get_barrier_semaphore()
    for to in ({"col": q_y}, {"row": mate}, {"row": across}, {"col": q_pair}):
        pl.semaphore_signal(barrier, inc=1, device_id=to, device_id_type=MESH)

    @pl.when(is_mid)
    def _():
        pl.semaphore_signal(barrier, inc=1, device_id={"col": q_mid}, device_id_type=MESH)

    cp_adj = pltpu.make_async_copy(adj_hbm, adj.at[pl.ds(0, slots)], lsem.at[0])
    cp_adj.start()
    cp_feat = pltpu.make_async_copy(feat_hbm, feat.at[0], lsem.at[1])
    cp_feat.start()
    w_mine = w_hbm.at[pl.ds(pl.multiple_of(p * quarter, quarter), quarter)]
    cp_w = pltpu.make_async_copy(w_mine, wfull.at[q, p], lsem.at[2])
    cp_w.start()

    def copy_to(src, dst, ssem, rsem, **to):
        return pltpu.make_async_remote_copy(
            src_ref=src, dst_ref=dst, send_sem=ssem, recv_sem=rsem, device_id=to, device_id_type=MESH)

    f_mate = copy_to(feat_hbm, feat.at[1], fsend.at[0], frecv.at[0], row=mate)
    f_across = copy_to(feat_hbm, feat.at[2], fsend.at[1], frecv.at[1], row=across)
    f_fwd = copy_to(feat.at[2], feat.at[3], fsend.at[2], frecv.at[2], row=mate)
    v_mate = copy_to(wfull.at[:, p], wfull.at[:, p], vsend.at[0], vrecv.at[0], row=mate)
    v_across = copy_to(wfull.at[:, p], wfull.at[:, p], vsend.at[1], vrecv.at[1], row=across)
    v_fwd = copy_to(wfull.at[:, across], wfull.at[:, across], vsend.at[2], vrecv.at[2], row=mate)

    def w_copy(n, ref, to):
        return copy_to(ref, ref, wsend.at[n], wrecv.at[n], col=to)

    def w_block(at_q):
        return wfull.at[at_q, p]

    def w_blocks(first, count):
        return wfull.at[pl.ds(first, count), p]

    w_up = w_copy(0, w_block(q), q_pair)
    w_own_y = w_copy(1, w_block(q), q_y)
    w_end_y = w_copy(2, w_block(q_pair), q_y)
    w_mids = w_copy(3, w_blocks(2 * z, 2), q_pair)
    w_end = w_copy(4, w_block(2 * pair_z + 1 - y), q_pair)
    w_half = w_copy(5, w_blocks(2 * z, 2), q_mid)
    w_half_end = w_copy(7, w_block(q_pair), q_mid)
    w_half_last = w_copy(8, w_block(2 * pair_z + 1 - y), q_mid)
    w_other = w_copy(6, w_blocks(4 - 4 * half, 4), q_pair)
    r_up = w_copy(0, w_block(q_pair), q_pair)
    r_own_y = w_copy(1, w_block(q_y), q_y)
    r_end_y = w_copy(2, w_block(2 * pair_z + 1 - y), q_y)
    r_mids = w_copy(3, w_blocks(2 * pair_z, 2), q_pair)
    r_end = w_copy(4, w_block(q_y), q_pair)
    r_half = w_copy(5, w_blocks(6 - 2 * z, 2), q_mid)
    r_half_end = w_copy(7, w_block(2 * (3 - pair_z) + y), q_mid)
    r_half_last = w_copy(8, w_block(2 * (3 - pair_z) + 1 - y), q_mid)
    r_other = w_copy(6, w_blocks(4 - 4 * half, 4), q_pair)

    def y_copy(k, i):
        d = at(i)
        return copy_to(psend.at[k, d], yr.at[k, d], ysend.at[k, d], yrecv.at[k, d], col=q_y)

    def p_copy(k, i):
        d = at(i)
        return copy_to(own.at[k, d], zp.at[k, d], psem.at[k, d], prsem.at[k, d], col=q_pair)

    def m_copy(k, i):
        d = at(i)
        return copy_to(own.at[k, d], zm.at[k, d], msem.at[k, d], mrsem.at[k, d], col=q_mid)

    g_copy = copy_to(psend.at[3, at(2)], mb, gsem.at[0], gsem.at[1], col=q_mid)

    def b_copy(k):
        return copy_to(psend.at[k, at(0)], zb.at[k], bsend.at[k], brecv.at[k], col=q_pair)

    def densify(side, d):
        base = (2 * d + side) * 16
        for up in range(2):
            for cb in range(8):
                dense[side, d, up * tb:(up + 1) * tb, cb * tb:(cb + 1) * tb] = adj[inv[base + up * 8 + cb]]

    def product(k, side, d):
        return jnp.dot(dense[side, d], feat[k], preferred_element_type=jnp.float32).astype(jnp.bfloat16)

    def total(refs):
        out = refs[0][...].astype(jnp.float32)
        for ref in refs[1:]:
            out = out + ref[...].astype(jnp.float32)
        return out.astype(jnp.bfloat16)

    def add_end(k, i):
        d = at(i)
        y_copy(k, i).wait_recv()
        own[k, d] = total([own.at[k, d], yr.at[k, d]])
        p_copy(k, i).start()

    def add_mid(k, i):
        d = at(i)
        p_copy(k, i).wait_recv()
        if (k, i) == (3, 2):
            own[k, d] = total([own.at[k, d], zp.at[k, d]])
        else:
            y_copy(k, i).wait_recv()
            own[k, d] = total([own.at[k, d], yr.at[k, d], zp.at[k, d]])
        m_copy(k, i).start()

    def add_out(k):
        d = at(0)
        m_copy(k, 0).wait_recv()
        if k < 2:
            y_copy(k, 0).wait_recv()
            own[k, d] = total([own.at[k, d], yr.at[k, d], zm.at[k, d]])
        else:
            own[k, d] = total([own.at[k, d], zm.at[k, d]])
        p_copy(k, 0).start()

    def merge(k):
        d = at(0)
        b_copy(k).wait_recv()
        psend[k, d] = total([psend.at[k, d], zb.at[k]])
        y_copy(k, 0).start()

    def settle(k):
        @pl.when(is_end)
        def _():
            p_copy(k, 0).wait_recv()
            if k < 2:
                acc[...] = total([own.at[k, z], zp.at[k, z]])
            else:
                y_copy(k, 0).wait_recv()
                acc[...] = total([own.at[k, z], zp.at[k, z], yr.at[k, z]])

        @pl.when(is_mid)
        def _():
            y_copy(k, 1).wait_recv()
            m_copy(k, 1).wait_recv()
            p_copy(k, 1).wait_recv()
            acc[...] = total([own.at[k, z], yr.at[k, z], zm.at[k, z], zp.at[k, z]])

    panels = (p, mate, across, (mate + 2) % 4)

    def finish(k):
        settle(k)
        rows = wfull[pl.ds(2 * panels[k], 2)].reshape(8 * quarter, wfull.shape[3])
        term = jnp.dot(acc[...], rows, preferred_element_type=jnp.float32)
        if k == 0:
            hidden[...] = term
        elif k < 3:
            hidden[...] += term
        else:
            out_ref[...] = jnp.maximum(hidden[...] + term, 0.0).astype(jnp.bfloat16)

    adj[slots] = jnp.zeros((tb, tb), jnp.bfloat16)
    cp_w.wait()
    pl.semaphore_wait(barrier, 4 + (z + 1) % 4 // 2)

    @pl.when(is_end)
    def _():
        w_up.start()

    @pl.when(is_mid)
    def _():
        w_own_y.start()

    f_mate.start()
    f_across.start()
    cp_adj.wait()
    cp_feat.wait()

    @pl.loop(0, 4)
    def _(step):
        d = at(3 - step)
        densify(1 - y, d)
        psend[0, d] = product(0, 1 - y, d)

        @pl.when(step < 2)
        def _():
            y_copy(0, 3 - step).start()

    @pl.when(is_end)
    def _():
        b_copy(0).start()

    @pl.when(is_mid)
    def _():
        r_up.wait_recv()
        w_end_y.start()
        w_half_end.start()
        r_own_y.wait_recv()
        w_half.start()
        w_mids.start()

    f_mate.wait_recv()

    @pl.loop(0, 4)
    def _(step):
        d = at(3 - step)
        psend[1, d] = product(1, 1 - y, d)

        @pl.when(step < 2)
        def _():
            y_copy(1, 3 - step).start()

    y_copy(0, 1).start()

    @pl.when(is_end)
    def _():
        b_copy(1).start()
        y_copy(1, 1).start()

    @pl.loop(0, 4)
    def _(step):
        d = at(3 - step)
        densify(y, d)
        own[0, d] = product(0, y, d)
        own[1, d] = product(1, y, d)

    @pl.when(is_end)
    def _():
        add_end(0, 3)
        add_end(0, 2)
        add_end(1, 3)
        add_end(1, 2)

    @pl.when(is_mid)
    def _():
        merge(0)
        merge(1)
        y_copy(1, 1).start()
        r_end_y.wait_recv()
        w_end.start()
        w_half_last.start()
        add_mid(0, 3)

    f_across.wait_recv()
    f_fwd.start()

    @pl.loop(0, 4)
    def _(step):
        d = at(3 - step)
        psend[2, d] = product(2, 1 - y, d)

        @pl.when(step == 0)
        def _():
            y_copy(2, 3).start()

    @pl.when(is_mid)
    def _():
        b_copy(2).start()
        r_half_end.wait_recv()
        r_half.wait_recv()
        r_half_last.wait_recv()
        w_other.start()
        add_mid(0, 2)

    f_fwd.wait_recv()

    @pl.loop(0, 4)
    def _(step):
        d = at(3 - step)
        psend[3, d] = product(3, 1 - y, d)

        @pl.when(step == 0)
        def _():
            y_copy(3, 3).start()
            y_copy(2, 2).start()

    @pl.when(is_end)
    def _():
        y_copy(3, 2).start()
        y_copy(2, 1).start()
        y_copy(3, 1).start()
        add_end(0, 1)

    @pl.when(is_mid)
    def _():
        y_copy(2, 1).start()
        g_copy.start()
        b_copy(3).start()
        v_across.start()
        v_mate.start()

    @pl.loop(0, 4)
    def _(step):
        d = at(3 - step)
        own[2, d] = product(2, y, d)
        own[3, d] = product(3, y, d)

    @pl.when(is_end)
    def _():
        add_end(1, 1)
        r_mids.wait_recv()
        r_end.wait_recv()
        r_other.wait_recv()
        v_across.start()
        v_mate.start()
        add_end(2, 3)
        merge(2)
        merge(3)
        add_end(3, 3)
        add_end(2, 2)
        add_end(3, 2)

    @pl.when(is_mid)
    def _():
        add_mid(1, 3)
        add_out(0)
        g_copy.wait_recv()
        psend[3, at(1)] = total([psend.at[3, at(1)], mb])
        y_copy(3, 1).start()
        add_mid(1, 2)
        add_out(1)
        add_mid(2, 3)
        add_mid(3, 3)

    v_across.wait_recv()
    v_fwd.start()

    @pl.when(is_end)
    def _():
        add_end(2, 1)

    @pl.when(is_mid)
    def _():
        add_out(2)
        add_mid(2, 2)

    v_mate.wait_recv()
    v_fwd.wait_recv()
    finish(0)
    finish(1)

    @pl.when(is_end)
    def _():
        add_end(3, 1)

    @pl.when(is_mid)
    def _():
        add_out(3)
        add_mid(3, 2)

    finish(2)
    finish(3)

    for copy in (f_mate, f_across, f_fwd, v_mate, v_across, v_fwd):
        copy.wait_send()

    @pl.loop(0, 4)
    def _(k):
        for i in (1, 3):
            y_copy(k, i).wait_send()

    @pl.loop(0, 3)
    def _(k):
        y_copy(k, 2).wait_send()

    @pl.when(is_end)
    def _():
        w_up.wait_send()
        y_copy(3, 2).wait_send()
        for k in (0, 1):
            b_copy(k).wait_send()
            y_copy(k + 2, 0).wait_send()

        @pl.loop(0, 4)
        def _(k):
            for i in (1, 2, 3):
                p_copy(k, i).wait_send()

    @pl.when(is_mid)
    def _():
        for copy in (w_own_y, w_end_y, w_mids, w_end, w_half, w_half_end, w_half_last, w_other, g_copy):
            copy.wait_send()
        for k in (0, 1):
            b_copy(k + 2).wait_send()
            y_copy(k, 0).wait_send()

        @pl.loop(0, 4)
        def _(k):
            p_copy(k, 0).wait_send()
            m_copy(k, 3).wait_send()
            m_copy(k, 2).wait_send()


def fused_shards(adjacency_tiles, tile_rows, tile_cols, tile_counts, features, weight):
    tiles = adjacency_tiles[0, 0]
    slots, tb = tiles.shape[:2]
    live = jnp.arange(slots, dtype=jnp.int32)
    key = tile_rows[0, 0] * 8 + tile_cols[0, 0]
    place = jnp.arange(128, dtype=jnp.int32)
    hit = (place[:, None] == key[None, :]) & (live[None, :] < tile_counts[0, 0])
    inv = jnp.min(jnp.where(hit, live[None, :], slots), axis=1)
    width = features.shape[1]
    wide = weight.shape[1]
    bf = jnp.bfloat16
    dma = pltpu.SemaphoreType.DMA
    blocks = (4, 4, 256, width)
    return pl.pallas_call(
        layer_kernel,
        out_shape=jax.ShapeDtypeStruct((256, wide), bf),
        in_specs=[pl.BlockSpec(memory_space=pltpu.SMEM)]
        + [pl.BlockSpec(memory_space=pltpu.HBM)] * 3,
        out_specs=pl.BlockSpec(memory_space=pltpu.VMEM),
        scratch_shapes=[
            pltpu.VMEM((slots + 1, tb, tb), bf),
            pltpu.VMEM((2, 4, 256, 1024), bf),
            pltpu.VMEM((4, 1024, width), bf),
            pltpu.VMEM((8, 4, weight.shape[0] // 4, wide), bf),
            pltpu.VMEM(blocks, bf),
            pltpu.VMEM(blocks, bf),
            pltpu.VMEM(blocks, bf),
            pltpu.VMEM(blocks, bf),
            pltpu.VMEM(blocks, bf),
            pltpu.VMEM((4, 256, width), bf),
            pltpu.VMEM((256, width), bf),
            pltpu.VMEM((256, width), bf),
            pltpu.VMEM((256, wide), jnp.float32),
            dma((3,)),
            dma((3,)), dma((3,)),
            dma((9,)), dma((9,)),
            dma((3,)), dma((3,)),
            dma((4, 4)), dma((4, 4)),
            dma((4, 4)), dma((4, 4)),
            dma((4, 4)), dma((4, 4)),
            dma((4,)), dma((4,)),
            dma((2,)),
        ],
        compiler_params=pltpu.CompilerParams(
            collective_id=0, has_side_effects=True, vmem_limit_bytes=48 * 2**20),
    )(inv, *(pltpu.with_memory_space_constraint(a, pltpu.HBM) for a in (tiles, features, weight)))


def solution(mesh):
    fits = mesh.shape["row"] == 4 and mesh.shape["col"] == 8
    return jax.shard_map(
        fused_shards if fits else shards,
        mesh=mesh,
        in_specs=(
            P("row", "col", None, None, None),
            P("row", "col", None),
            P("row", "col", None),
            P("row", "col"),
            P("col", "row"),
            P("col", None),
        ),
        out_specs=P(("row", "col"), None),
        check_vma=False,
    )
```

```python
import functools

import jax
import jax.numpy as jnp
from jax import lax
from jax.experimental import pallas as pl
from jax.experimental.pallas import tpu as pltpu
from jax.sharding import PartitionSpec as P

MESH = pl.DeviceIdType.MESH


def densify(adjacency_tiles, tile_rows, tile_cols, tile_count, row_blocks, column_blocks):
    slots = adjacency_tiles.shape[0]
    tile_edge = adjacency_tiles.shape[1]
    live_mask = (jnp.arange(slots, dtype=jnp.int32) < tile_count).astype(jnp.bfloat16)
    masked = adjacency_tiles * live_mask[:, None, None]
    grid = jnp.zeros((row_blocks, column_blocks, tile_edge, tile_edge), jnp.bfloat16)
    grid = grid.at[tile_rows, tile_cols].add(masked)
    return grid.transpose(0, 2, 1, 3).reshape(row_blocks * tile_edge, column_blocks * tile_edge)


def reduce_whole(partial_rows):
    return lax.psum_scatter(
        partial_rows.astype(jnp.bfloat16), "col", scatter_dimension=0, tiled=True
    ).astype(jnp.float32)


def shards(adjacency_tiles, tile_rows, tile_cols, tile_counts, features, weight):
    local_tiles = adjacency_tiles[0, 0]
    local_rows = tile_rows[0, 0]
    local_cols = tile_cols[0, 0]
    local_count = tile_counts[0, 0]
    tile_edge = local_tiles.shape[1]
    column_blocks = features.shape[0] // tile_edge
    row_blocks = column_blocks * lax.axis_size("col") // lax.axis_size("row")
    dense_block = densify(
        local_tiles, local_rows, local_cols, local_count, row_blocks, column_blocks
    )
    whole = lax.all_gather(features, "row", axis=1, tiled=True)
    partial_value = jnp.dot(dense_block, whole, preferred_element_type=jnp.float32)
    summed = reduce_whole(partial_value.astype(jnp.bfloat16).astype(jnp.float32))
    aggregated = summed.astype(jnp.bfloat16)
    full_weight = lax.all_gather(weight, "col", axis=0, tiled=True)
    hidden = jnp.dot(aggregated, full_weight, preferred_element_type=jnp.float32)
    return jnp.maximum(hidden, 0.0).astype(jnp.bfloat16)


def layer_kernel(
    count, rows_hbm, cols_hbm, adj_hbm, feat_hbm, w_hbm, out_ref,
    table, inv_lanes, inv, adj, dense, feat, wfull, psend, own, yr, zp, zm, zb, mb, acc, hidden,
    lsem, fsend, frecv, wsend, wrecv, vsend, vrecv, ysend, yrecv, psem, prsem, msem, mrsem, bsend, brecv, gsem,
):
    p, q = lax.axis_index("row"), lax.axis_index("col")
    y, z = q % 2, q // 2
    mate = p + 1 - 2 * (p % 2)
    across = (p + 2) % 4
    half = z // 2
    pair_z = z + 1 - 2 * (z % 2)
    q_y, q_pair, q_mid = 2 * z + 1 - y, 2 * pair_z + y, 2 * (3 - z) + y
    is_end = z % 3 == 0
    is_mid = z % 3 > 0
    slots = adj_hbm.shape[0]
    tb = adj_hbm.shape[1]
    quarter = wfull.shape[2]

    def at(i):
        return i + half * (3 - 2 * i)

    barrier = pltpu.get_barrier_semaphore()
    for to in ({"col": q_y}, {"row": mate}, {"row": across}, {"col": q_pair}):
        pl.semaphore_signal(barrier, inc=1, device_id=to, device_id_type=MESH)

    @pl.when(is_mid)
    def _():
        pl.semaphore_signal(barrier, inc=1, device_id={"col": q_mid}, device_id_type=MESH)

    cp_table = [
        pltpu.make_async_copy(ref, table.at[n], lsem.at[3 + n])
        for n, ref in enumerate((rows_hbm, cols_hbm))
    ]
    for copy in cp_table:
        copy.start()
    cp_adj = pltpu.make_async_copy(adj_hbm, adj.at[pl.ds(0, slots)], lsem.at[0])
    cp_adj.start()
    cp_feat = pltpu.make_async_copy(feat_hbm, feat.at[0], lsem.at[1])
    cp_feat.start()
    w_mine = w_hbm.at[pl.ds(pl.multiple_of(p * quarter, quarter), quarter)]
    cp_w = pltpu.make_async_copy(w_mine, wfull.at[q, p], lsem.at[2])
    cp_w.start()

    def copy_to(src, dst, ssem, rsem, **to):
        return pltpu.make_async_remote_copy(
            src_ref=src, dst_ref=dst, send_sem=ssem, recv_sem=rsem, device_id=to, device_id_type=MESH)

    f_mate = copy_to(feat_hbm, feat.at[1], fsend.at[0], frecv.at[0], row=mate)
    f_across = copy_to(feat_hbm, feat.at[2], fsend.at[1], frecv.at[1], row=across)
    f_fwd = copy_to(feat.at[2], feat.at[3], fsend.at[2], frecv.at[2], row=mate)
    v_mate = copy_to(wfull.at[:, p], wfull.at[:, p], vsend.at[0], vrecv.at[0], row=mate)
    v_across = copy_to(wfull.at[:, p], wfull.at[:, p], vsend.at[1], vrecv.at[1], row=across)
    v_fwd = copy_to(wfull.at[:, across], wfull.at[:, across], vsend.at[2], vrecv.at[2], row=mate)

    def w_copy(n, ref, to):
        return copy_to(ref, ref, wsend.at[n], wrecv.at[n], col=to)

    def w_block(at_q):
        return wfull.at[at_q, p]

    def w_blocks(first, count):
        return wfull.at[pl.ds(first, count), p]

    w_up = w_copy(0, w_block(q), q_pair)
    w_own_y = w_copy(1, w_block(q), q_y)
    w_end_y = w_copy(2, w_block(q_pair), q_y)
    w_mids = w_copy(3, w_blocks(2 * z, 2), q_pair)
    w_end = w_copy(4, w_block(2 * pair_z + 1 - y), q_pair)
    w_half = w_copy(5, w_blocks(2 * z, 2), q_mid)
    w_half_end = w_copy(7, w_block(q_pair), q_mid)
    w_half_last = w_copy(8, w_block(2 * pair_z + 1 - y), q_mid)
    w_other = w_copy(6, w_blocks(4 - 4 * half, 4), q_pair)
    r_up = w_copy(0, w_block(q_pair), q_pair)
    r_own_y = w_copy(1, w_block(q_y), q_y)
    r_end_y = w_copy(2, w_block(2 * pair_z + 1 - y), q_y)
    r_mids = w_copy(3, w_blocks(2 * pair_z, 2), q_pair)
    r_end = w_copy(4, w_block(q_y), q_pair)
    r_half = w_copy(5, w_blocks(6 - 2 * z, 2), q_mid)
    r_half_end = w_copy(7, w_block(2 * (3 - pair_z) + y), q_mid)
    r_half_last = w_copy(8, w_block(2 * (3 - pair_z) + 1 - y), q_mid)
    r_other = w_copy(6, w_blocks(4 - 4 * half, 4), q_pair)

    def y_copy(k, i):
        d = at(i)
        return copy_to(psend.at[k, d], yr.at[k, d], ysend.at[k, d], yrecv.at[k, d], col=q_y)

    def p_copy(k, i):
        d = at(i)
        return copy_to(own.at[k, d], zp.at[k, d], psem.at[k, d], prsem.at[k, d], col=q_pair)

    def m_copy(k, i):
        d = at(i)
        return copy_to(own.at[k, d], zm.at[k, d], msem.at[k, d], mrsem.at[k, d], col=q_mid)

    g_copy = copy_to(psend.at[3, at(2)], mb, gsem.at[0], gsem.at[1], col=q_mid)

    def b_copy(k):
        return copy_to(psend.at[k, at(0)], zb.at[k], bsend.at[k], brecv.at[k], col=q_pair)

    def densify(side, d):
        base = (2 * d + side) * 16
        for up in range(2):
            for cb in range(8):
                dense[side, d, up * tb:(up + 1) * tb, cb * tb:(cb + 1) * tb] = adj[inv[0, base + up * 8 + cb]]

    def product(k, side, d):
        return jnp.dot(dense[side, d], feat[k], preferred_element_type=jnp.float32).astype(jnp.bfloat16)

    def total(refs):
        out = refs[0][...].astype(jnp.float32)
        for ref in refs[1:]:
            out = out + ref[...].astype(jnp.float32)
        return out.astype(jnp.bfloat16)

    def add_end(k, i):
        d = at(i)
        y_copy(k, i).wait_recv()
        own[k, d] = total([own.at[k, d], yr.at[k, d]])
        p_copy(k, i).start()

    def add_mid(k, i):
        d = at(i)
        p_copy(k, i).wait_recv()
        if (k, i) == (3, 2):
            own[k, d] = total([own.at[k, d], zp.at[k, d]])
        else:
            y_copy(k, i).wait_recv()
            own[k, d] = total([own.at[k, d], yr.at[k, d], zp.at[k, d]])
        m_copy(k, i).start()

    def add_out(k):
        d = at(0)
        m_copy(k, 0).wait_recv()
        if k < 2:
            y_copy(k, 0).wait_recv()
            own[k, d] = total([own.at[k, d], yr.at[k, d], zm.at[k, d]])
        else:
            own[k, d] = total([own.at[k, d], zm.at[k, d]])
        p_copy(k, 0).start()

    def merge(k):
        d = at(0)
        b_copy(k).wait_recv()
        psend[k, d] = total([psend.at[k, d], zb.at[k]])
        y_copy(k, 0).start()

    def settle(k):
        @pl.when(is_end)
        def _():
            p_copy(k, 0).wait_recv()
            if k < 2:
                acc[...] = total([own.at[k, z], zp.at[k, z]])
            else:
                y_copy(k, 0).wait_recv()
                acc[...] = total([own.at[k, z], zp.at[k, z], yr.at[k, z]])

        @pl.when(is_mid)
        def _():
            y_copy(k, 1).wait_recv()
            m_copy(k, 1).wait_recv()
            p_copy(k, 1).wait_recv()
            acc[...] = total([own.at[k, z], yr.at[k, z], zm.at[k, z], zp.at[k, z]])

    panels = (p, mate, across, (mate + 2) % 4)

    def finish(k):
        settle(k)
        rows = wfull[pl.ds(2 * panels[k], 2)].reshape(8 * quarter, wfull.shape[3])
        term = jnp.dot(acc[...], rows, preferred_element_type=jnp.float32)
        if k == 0:
            hidden[...] = term
        elif k < 3:
            hidden[...] += term
        else:
            out_ref[...] = jnp.maximum(hidden[...] + term, 0.0).astype(jnp.bfloat16)

    adj[slots] = jnp.zeros((tb, tb), jnp.bfloat16)
    for copy in cp_table:
        copy.wait()
    wide = (128, slots)
    slot = lax.broadcasted_iota(jnp.int32, wide, 1)
    key = jnp.broadcast_to(table[0] * 8 + table[1], wide)
    hit = (key == lax.broadcasted_iota(jnp.int32, wide, 0)) & (slot < count[0, 0])
    found = jnp.min(jnp.where(hit, slot, slots), axis=1, keepdims=True)
    square = (128, 128)
    diagonal = lax.broadcasted_iota(jnp.int32, square, 0) == lax.broadcasted_iota(jnp.int32, square, 1)
    inv_lanes[...] = jnp.min(jnp.where(diagonal, found, slots), axis=0, keepdims=True)
    cp_inv = pltpu.make_async_copy(inv_lanes, inv, lsem.at[5])
    cp_inv.start()

    cp_w.wait()
    pl.semaphore_wait(barrier, 4 + (z + 1) % 4 // 2)

    @pl.when(is_end)
    def _():
        w_up.start()

    @pl.when(is_mid)
    def _():
        w_own_y.start()

    f_mate.start()
    f_across.start()
    cp_inv.wait()
    cp_adj.wait()
    cp_feat.wait()

    @pl.loop(0, 4)
    def _(step):
        i = (4 - (z + 1) % 4 // 2 - step) % 4
        d = at(i)
        densify(1 - y, d)
        psend[0, d] = product(0, 1 - y, d)

        @pl.when(i >= 2)
        def _():
            y_copy(0, i).start()

        @pl.when(is_end & (i == 0))
        def _():
            b_copy(0).start()

    @pl.when(is_mid)
    def _():
        r_up.wait_recv()
        w_end_y.start()
        w_half_end.start()
        r_own_y.wait_recv()
        w_half.start()
        w_mids.start()

    f_mate.wait_recv()

    @pl.loop(0, 4)
    def _(step):
        i = (4 - (z + 1) % 4 // 2 - step) % 4
        d = at(i)
        psend[1, d] = product(1, 1 - y, d)

        @pl.when(i >= 2)
        def _():
            y_copy(1, i).start()

        @pl.when(is_end & (i == 0))
        def _():
            b_copy(1).start()

    y_copy(0, 1).start()

    @pl.loop(0, 4)
    def _(step):
        d = at(3 - step)
        densify(y, d)
        own[0, d] = product(0, y, d)
        own[1, d] = product(1, y, d)

    @pl.when(is_end)
    def _():
        add_end(0, 3)
        add_end(0, 2)
        add_end(1, 3)

    @pl.when(is_mid)
    def _():
        merge(0)
        r_end_y.wait_recv()
        w_end.start()
        w_half_last.start()
        add_mid(0, 3)

    f_across.wait_recv()
    f_fwd.start()

    @pl.loop(0, 4)
    def _(step):
        d = at(3 - step)
        psend[2, d] = product(2, 1 - y, d)

        @pl.when(step == 0)
        def _():
            y_copy(2, 3).start()

    @pl.when(is_end)
    def _():
        add_end(1, 2)

    @pl.when(is_mid)
    def _():
        b_copy(2).start()
        r_half_end.wait_recv()
        r_half.wait_recv()
        r_half_last.wait_recv()
        w_other.start()
        add_mid(0, 2)

    f_fwd.wait_recv()

    @pl.loop(0, 4)
    def _(step):
        d = at(3 - step)
        psend[3, d] = product(3, 1 - y, d)

        @pl.when(step == 0)
        def _():
            y_copy(3, 3).start()
            y_copy(2, 2).start()

    @pl.when(is_end)
    def _():
        y_copy(3, 2).start()
        y_copy(1, 1).start()
        y_copy(2, 1).start()
        y_copy(3, 1).start()
        add_end(0, 1)

    @pl.when(is_mid)
    def _():
        g_copy.start()
        merge(1)
        y_copy(1, 1).start()
        y_copy(2, 1).start()
        b_copy(3).start()
        v_across.start()
        v_mate.start()

    @pl.loop(0, 4)
    def _(step):
        d = at(3 - step)
        own[2, d] = product(2, y, d)
        own[3, d] = product(3, y, d)

    @pl.when(is_end)
    def _():
        add_end(2, 3)
        r_mids.wait_recv()
        r_end.wait_recv()
        r_other.wait_recv()
        v_across.start()
        v_mate.start()
        add_end(3, 3)
        merge(2)
        merge(3)
        add_end(2, 2)
        add_end(3, 2)
        add_end(1, 1)

    @pl.when(is_mid)
    def _():
        add_mid(1, 3)
        add_out(0)
        g_copy.wait_recv()
        psend[3, at(1)] = total([psend.at[3, at(1)], mb])
        y_copy(3, 1).start()
        add_mid(1, 2)
        add_mid(2, 3)
        add_mid(3, 3)
        add_mid(2, 2)

    v_across.wait_recv()
    v_fwd.start()

    @pl.when(is_end)
    def _():
        add_end(2, 1)

    @pl.when(is_mid)
    def _():
        add_out(1)
        add_mid(3, 2)
        add_out(2)

    v_mate.wait_recv()
    v_fwd.wait_recv()
    finish(0)

    @pl.when(is_end)
    def _():
        add_end(3, 1)

    @pl.when(is_mid)
    def _():
        add_out(3)

    finish(1)
    finish(2)
    finish(3)

    for copy in (f_mate, f_across, f_fwd, v_mate, v_across, v_fwd):
        copy.wait_send()

    @pl.loop(0, 4)
    def _(k):
        for i in (1, 3):
            y_copy(k, i).wait_send()

    @pl.loop(0, 3)
    def _(k):
        y_copy(k, 2).wait_send()

    @pl.when(is_end)
    def _():
        w_up.wait_send()
        y_copy(3, 2).wait_send()
        for k in (0, 1):
            b_copy(k).wait_send()
            y_copy(k + 2, 0).wait_send()

        @pl.loop(0, 4)
        def _(k):
            for i in (1, 2, 3):
                p_copy(k, i).wait_send()

    @pl.when(is_mid)
    def _():
        for copy in (w_own_y, w_end_y, w_mids, w_end, w_half, w_half_end, w_half_last, w_other, g_copy):
            copy.wait_send()
        for k in (0, 1):
            b_copy(k + 2).wait_send()
            y_copy(k, 0).wait_send()

        @pl.loop(0, 4)
        def _(k):
            p_copy(k, 0).wait_send()
            m_copy(k, 3).wait_send()
            m_copy(k, 2).wait_send()


def fused_shards(adjacency_tiles, tile_rows, tile_cols, tile_counts, features, weight):
    tiles = adjacency_tiles[0, 0]
    slots, tb = tiles.shape[:2]
    width = features.shape[1]
    wide = weight.shape[1]
    bf = jnp.bfloat16
    dma = pltpu.SemaphoreType.DMA
    blocks = (4, 4, 256, width)
    return pl.pallas_call(
        layer_kernel,
        out_shape=jax.ShapeDtypeStruct((256, wide), bf),
        in_specs=[pl.BlockSpec(memory_space=pltpu.SMEM)]
        + [pl.BlockSpec(memory_space=pltpu.HBM)] * 5,
        out_specs=pl.BlockSpec(memory_space=pltpu.VMEM),
        scratch_shapes=[
            pltpu.VMEM((2, 1, slots), jnp.int32),
            pltpu.VMEM((1, 128), jnp.int32),
            pltpu.SMEM((1, 128), jnp.int32),
            pltpu.VMEM((slots + 1, tb, tb), bf),
            pltpu.VMEM((2, 4, 256, 1024), bf),
            pltpu.VMEM((4, 1024, width), bf),
            pltpu.VMEM((8, 4, weight.shape[0] // 4, wide), bf),
            pltpu.VMEM(blocks, bf),
            pltpu.VMEM(blocks, bf),
            pltpu.VMEM(blocks, bf),
            pltpu.VMEM(blocks, bf),
            pltpu.VMEM(blocks, bf),
            pltpu.VMEM((4, 256, width), bf),
            pltpu.VMEM((256, width), bf),
            pltpu.VMEM((256, width), bf),
            pltpu.VMEM((256, wide), jnp.float32),
            dma((6,)),
            dma((3,)), dma((3,)),
            dma((9,)), dma((9,)),
            dma((3,)), dma((3,)),
            dma((4, 4)), dma((4, 4)),
            dma((4, 4)), dma((4, 4)),
            dma((4, 4)), dma((4, 4)),
            dma((4,)), dma((4,)),
            dma((2,)),
        ],
        compiler_params=pltpu.CompilerParams(
            collective_id=0, has_side_effects=True, vmem_limit_bytes=48 * 2**20),
    )(tile_counts, *(pltpu.with_memory_space_constraint(a, pltpu.HBM)
                     for a in (tile_rows[0], tile_cols[0], tiles, features, weight)))


def solution(mesh):
    fits = mesh.shape["row"] == 4 and mesh.shape["col"] == 8
    return jax.shard_map(
        fused_shards if fits else shards,
        mesh=mesh,
        in_specs=(
            P("row", "col", None, None, None),
            P("row", "col", None),
            P("row", "col", None),
            P("row", "col"),
            P("col", "row"),
            P("col", None),
        ),
        out_specs=P(("row", "col"), None),
        check_vma=False,
    )
```

```python
import functools

import jax
import jax.numpy as jnp
from jax import lax
from jax.experimental import pallas as pl
from jax.experimental.pallas import tpu as pltpu
from jax.sharding import PartitionSpec as P

MESH = pl.DeviceIdType.MESH


def densify(adjacency_tiles, tile_rows, tile_cols, tile_count, row_blocks, column_blocks):
    slots = adjacency_tiles.shape[0]
    tile_edge = adjacency_tiles.shape[1]
    live_mask = (jnp.arange(slots, dtype=jnp.int32) < tile_count).astype(jnp.bfloat16)
    masked = adjacency_tiles * live_mask[:, None, None]
    grid = jnp.zeros((row_blocks, column_blocks, tile_edge, tile_edge), jnp.bfloat16)
    grid = grid.at[tile_rows, tile_cols].add(masked)
    return grid.transpose(0, 2, 1, 3).reshape(row_blocks * tile_edge, column_blocks * tile_edge)


def reduce_whole(partial_rows):
    return lax.psum_scatter(
        partial_rows.astype(jnp.bfloat16), "col", scatter_dimension=0, tiled=True
    ).astype(jnp.float32)


def shards(adjacency_tiles, tile_rows, tile_cols, tile_counts, features, weight):
    local_tiles = adjacency_tiles[0, 0]
    local_rows = tile_rows[0, 0]
    local_cols = tile_cols[0, 0]
    local_count = tile_counts[0, 0]
    tile_edge = local_tiles.shape[1]
    column_blocks = features.shape[0] // tile_edge
    row_blocks = column_blocks * lax.axis_size("col") // lax.axis_size("row")
    dense_block = densify(
        local_tiles, local_rows, local_cols, local_count, row_blocks, column_blocks
    )
    whole = lax.all_gather(features, "row", axis=1, tiled=True)
    partial_value = jnp.dot(dense_block, whole, preferred_element_type=jnp.float32)
    summed = reduce_whole(partial_value.astype(jnp.bfloat16).astype(jnp.float32))
    aggregated = summed.astype(jnp.bfloat16)
    full_weight = lax.all_gather(weight, "col", axis=0, tiled=True)
    hidden = jnp.dot(aggregated, full_weight, preferred_element_type=jnp.float32)
    return jnp.maximum(hidden, 0.0).astype(jnp.bfloat16)


def layer_kernel(
    count, rows_hbm, cols_hbm, adj_hbm, feat_hbm, w_hbm, out_ref,
    table, inv_lanes, inv, adj, dense, feat, wfull, psend, own, yr, zp, zm, zb, mb, base, acc, hidden,
    lsem, fsend, frecv, wsend, wrecv, vsend, vrecv, ysend, yrecv, psem, prsem, msem, mrsem, bsend, brecv, gsem, tsend, trecv,
):
    p, q = lax.axis_index("row"), lax.axis_index("col")
    y, z = q % 2, q // 2
    mate = p + 1 - 2 * (p % 2)
    across = (p + 2) % 4
    half = z // 2
    pair_z = z + 1 - 2 * (z % 2)
    q_y, q_pair, q_mid = 2 * z + 1 - y, 2 * pair_z + y, 2 * (3 - z) + y
    is_end = z % 3 == 0
    is_mid = z % 3 > 0
    more = half + y == 0
    less = (half == 0) & (y == 1)
    slots = adj_hbm.shape[0]
    tb = adj_hbm.shape[1]
    quarter = wfull.shape[2]

    def at(i):
        return i + half * (3 - 2 * i)

    barrier = pltpu.get_barrier_semaphore()
    for to in ({"col": q_y}, {"row": mate}, {"row": across}, {"col": q_pair}):
        pl.semaphore_signal(barrier, inc=1, device_id=to, device_id_type=MESH)

    @pl.when(is_mid)
    def _():
        pl.semaphore_signal(barrier, inc=1, device_id={"col": q_mid}, device_id_type=MESH)

    cp_table = [
        pltpu.make_async_copy(ref, table.at[n], lsem.at[3 + n])
        for n, ref in enumerate((rows_hbm, cols_hbm))
    ]
    for copy in cp_table:
        copy.start()
    cp_adj = pltpu.make_async_copy(adj_hbm, adj.at[pl.ds(0, slots)], lsem.at[0])
    cp_adj.start()
    cp_feat = pltpu.make_async_copy(feat_hbm, feat.at[0], lsem.at[1])
    cp_feat.start()
    w_mine = w_hbm.at[pl.ds(pl.multiple_of(p * quarter, quarter), quarter)]
    cp_w = pltpu.make_async_copy(w_mine, wfull.at[q, p], lsem.at[2])
    cp_w.start()

    def copy_to(src, dst, ssem, rsem, **to):
        return pltpu.make_async_remote_copy(
            src_ref=src, dst_ref=dst, send_sem=ssem, recv_sem=rsem, device_id=to, device_id_type=MESH)

    f_mate = copy_to(feat_hbm, feat.at[1], fsend.at[0], frecv.at[0], row=mate)
    f_across = copy_to(feat_hbm, feat.at[2], fsend.at[1], frecv.at[1], row=across)
    f_fwd = copy_to(feat.at[2], feat.at[3], fsend.at[2], frecv.at[2], row=mate)
    v_mate = copy_to(wfull.at[:, p], wfull.at[:, p], vsend.at[0], vrecv.at[0], row=mate)
    v_across = copy_to(wfull.at[:, p], wfull.at[:, p], vsend.at[1], vrecv.at[1], row=across)
    v_fwd = copy_to(wfull.at[:, across], wfull.at[:, across], vsend.at[2], vrecv.at[2], row=mate)

    def w_copy(n, ref, to):
        return copy_to(ref, ref, wsend.at[n], wrecv.at[n], col=to)

    def w_block(at_q):
        return wfull.at[at_q, p]

    def w_blocks(first, count):
        return wfull.at[pl.ds(first, count), p]

    w_up = w_copy(0, w_block(q), q_pair)
    w_own_y = w_copy(1, w_block(q), q_y)
    w_end_y = w_copy(2, w_block(q_pair), q_y)
    w_mids = w_copy(3, w_blocks(2 * z, 2), q_pair)
    w_end = w_copy(4, w_block(2 * pair_z + 1 - y), q_pair)
    w_half = w_copy(5, w_blocks(2 * z, 2), q_mid)
    w_half_end = w_copy(7, w_block(q_pair), q_mid)
    w_half_last = w_copy(8, w_block(2 * pair_z + 1 - y), q_mid)
    w_other = w_copy(6, w_blocks(6 - 2 * z, 2), q_pair)
    w_other_end = w_copy(9, w_block(2 * (3 - pair_z) + y), q_pair)
    w_other_last = w_copy(10, w_block(2 * (3 - pair_z) + 1 - y), q_pair)
    r_up = w_copy(0, w_block(q_pair), q_pair)
    r_own_y = w_copy(1, w_block(q_y), q_y)
    r_end_y = w_copy(2, w_block(2 * pair_z + 1 - y), q_y)
    r_mids = w_copy(3, w_blocks(2 * pair_z, 2), q_pair)
    r_end = w_copy(4, w_block(q_y), q_pair)
    r_half = w_copy(5, w_blocks(6 - 2 * z, 2), q_mid)
    r_half_end = w_copy(7, w_block(2 * (3 - pair_z) + y), q_mid)
    r_half_last = w_copy(8, w_block(2 * (3 - pair_z) + 1 - y), q_mid)
    r_other = w_copy(6, w_blocks(6 - 2 * pair_z, 2), q_pair)
    r_other_end = w_copy(9, w_block(2 * (3 - z) + y), q_pair)
    r_other_last = w_copy(10, w_block(2 * (3 - z) + 1 - y), q_pair)

    def y_copy(k, i):
        d = at(i)
        return copy_to(psend.at[k, d], yr.at[k, d], ysend.at[k, d], yrecv.at[k, d], col=q_y)

    def p_copy(k, i):
        d = at(i)
        return copy_to(own.at[k, d], zp.at[k, d], psem.at[k, d], prsem.at[k, d], col=q_pair)

    def m_copy(k, i):
        d = at(i)
        return copy_to(own.at[k, d], zm.at[k, d], msem.at[k, d], mrsem.at[k, d], col=q_mid)

    g_copy = copy_to(psend.at[3, at(2)], mb, gsem.at[0], gsem.at[1], col=q_mid)

    def b_copy(k):
        return copy_to(psend.at[k, at(0)], zb.at[k], bsend.at[k], brecv.at[k], col=q_pair)

    def part(lo):
        return pl.ds(lo, 128)

    def y_part(k, lo, ssem, rsem):
        d = at(0)
        return copy_to(psend.at[k, d, part(lo)], yr.at[k, d, part(lo)], ssem, rsem, col=q_y)

    def y_half(lo):
        return y_part(2, lo, ysend.at[2, at(0)], yrecv.at[2, at(0)])

    def b_half(lo):
        return copy_to(psend.at[2, at(0), part(lo)], zb.at[2, part(lo)], bsend.at[2], brecv.at[2], col=q_pair)

    def y_tail(lo):
        return y_part(3, lo, tsend.at[lo // 128], trecv.at[lo // 128])

    def p_tail(lo):
        d = at(1)
        return copy_to(own.at[3, d, part(lo)], zp.at[3, d, part(lo)], tsend.at[2 + lo // 128], trecv.at[2 + lo // 128], col=q_pair)

    def densify(side, d):
        base = (2 * d + side) * 16
        for up in range(2):
            for cb in range(8):
                dense[side, d, up * tb:(up + 1) * tb, cb * tb:(cb + 1) * tb] = adj[inv[0, base + up * 8 + cb]]

    def product(k, side, d):
        return jnp.dot(dense[side, d], feat[k], preferred_element_type=jnp.float32).astype(jnp.bfloat16)

    def total(refs):
        out = refs[0][...].astype(jnp.float32)
        for ref in refs[1:]:
            out = out + ref[...].astype(jnp.float32)
        return out.astype(jnp.bfloat16)

    def add_end(k, i):
        d = at(i)
        y_copy(k, i).wait_recv()
        own[k, d] = total([own.at[k, d], yr.at[k, d]])
        if (k, i) == (3, 1):
            p_tail(0).start()
            p_tail(128).start()
        else:
            p_copy(k, i).start()

    def add_mid(k, i):
        d = at(i)
        p_copy(k, i).wait_recv()
        if (k, i) == (3, 2):
            own[k, d] = total([own.at[k, d], zp.at[k, d]])
        else:
            y_copy(k, i).wait_recv()
            own[k, d] = total([own.at[k, d], yr.at[k, d], zp.at[k, d]])
        m_copy(k, i).start()

    def add_out(k):
        d = at(0)
        m_copy(k, 0).wait_recv()

        def with_y():
            y_copy(k, 0).wait_recv()
            own[k, d] = total([own.at[k, d], yr.at[k, d], zm.at[k, d]])

        def with_half():
            y_half(0).wait_recv()
            own[k, d, :128] = total([ref.at[k, d, part(0)] for ref in (own, yr, zm)])
            own[k, d, 128:] = total([ref.at[k, d, part(128)] for ref in (own, zm)])

        def without_y():
            own[k, d] = total([own.at[k, d], zm.at[k, d]])

        if k == 2:
            pl.when(more)(with_half)
            pl.when(jnp.logical_not(more))(without_y)
        elif k < 2:
            with_y()
        else:
            without_y()
        p_copy(k, 0).start()

    def merge(k):
        d = at(0)
        b_copy(k).wait_recv()
        psend[k, d] = total([psend.at[k, d], zb.at[k]])
        y_copy(k, 0).start()

    def merge_half(lo):
        d = at(0)
        b_half(lo).wait_recv()
        psend[2, d, lo:lo + 128] = total([psend.at[2, d, part(lo)], zb.at[2, part(lo)]])
        y_half(lo).start()

    def merge_tail():
        d = at(0)
        b_copy(3).wait_recv()
        psend[3, d] = total([psend.at[3, d], zb.at[3]])
        y_tail(0).start()
        y_tail(128).start()

    def settle(k):
        @pl.when(is_end)
        def _():
            p_copy(k, 0).wait_recv()

            def without_y():
                acc[...] = total([own.at[k, z], zp.at[k, z]])

            def with_half():
                acc[:128] = total([own.at[k, z, part(0)], zp.at[k, z, part(0)]])
                y_half(128).wait_recv()
                acc[128:] = total([ref.at[k, z, part(128)] for ref in (own, zp, yr)])

            def with_y():
                y_copy(k, 0).wait_recv()
                acc[...] = total([own.at[k, z], zp.at[k, z], yr.at[k, z]])

            if k == 2:
                pl.when(more)(with_half)
                pl.when(jnp.logical_not(more))(with_y)
            else:
                without_y()

        @pl.when(is_mid)
        def _():
            y_copy(k, 1).wait_recv()
            m_copy(k, 1).wait_recv()
            p_copy(k, 1).wait_recv()
            acc[...] = total([own.at[k, z], yr.at[k, z], zm.at[k, z], zp.at[k, z]])

    panels = (p, mate, across, (mate + 2) % 4)

    def weight_rows(k):
        return wfull[pl.ds(2 * panels[k], 2)].reshape(8 * quarter, wfull.shape[3])

    def finish(k):
        settle(k)
        term = jnp.dot(acc[...], weight_rows(k), preferred_element_type=jnp.float32)
        if k == 0:
            hidden[...] = term
        else:
            hidden[...] += term

    def finish_last():
        @pl.when(is_end)
        def _():
            p_copy(3, 0).wait_recv()
            base[...] = own[3, z].astype(jnp.float32) + zp[3, z].astype(jnp.float32)

        @pl.when(is_mid)
        def _():
            y_copy(3, 1).wait_recv()
            m_copy(3, 1).wait_recv()
            base[...] = (own[3, z].astype(jnp.float32) + yr[3, z].astype(jnp.float32)) + zm[3, z].astype(jnp.float32)

        for lo in (0, 128):
            rows = slice(lo, lo + 128)

            @pl.when(is_end)
            def _():
                y_tail(lo).wait_recv()
                acc[rows] = (base[rows] + yr[3, z, rows].astype(jnp.float32)).astype(jnp.bfloat16)

            @pl.when(is_mid)
            def _():
                p_tail(lo).wait_recv()
                acc[rows] = (base[rows] + zp[3, z, rows].astype(jnp.float32)).astype(jnp.bfloat16)

            term = jnp.dot(acc[rows], weight_rows(3), preferred_element_type=jnp.float32)
            out_ref[rows] = jnp.maximum(hidden[rows] + term, 0.0).astype(jnp.bfloat16)

    adj[slots] = jnp.zeros((tb, tb), jnp.bfloat16)
    for copy in cp_table:
        copy.wait()
    wide = (128, slots)
    slot = lax.broadcasted_iota(jnp.int32, wide, 1)
    key = jnp.broadcast_to(table[0] * 8 + table[1], wide)
    hit = (key == lax.broadcasted_iota(jnp.int32, wide, 0)) & (slot < count[0, 0])
    found = jnp.min(jnp.where(hit, slot, slots), axis=1, keepdims=True)
    square = (128, 128)
    diagonal = lax.broadcasted_iota(jnp.int32, square, 0) == lax.broadcasted_iota(jnp.int32, square, 1)
    inv_lanes[...] = jnp.min(jnp.where(diagonal, found, slots), axis=0, keepdims=True)
    cp_inv = pltpu.make_async_copy(inv_lanes, inv, lsem.at[5])
    cp_inv.start()

    cp_w.wait()
    pl.semaphore_wait(barrier, 4 + (z + 1) % 4 // 2)

    @pl.when(is_end)
    def _():
        w_up.start()

    @pl.when(is_mid)
    def _():
        w_own_y.start()

    f_mate.start()
    f_across.start()
    cp_inv.wait()
    cp_adj.wait()
    cp_feat.wait()

    @pl.loop(0, 4)
    def _(step):
        i = (4 - (z + 1) % 4 // 2 - step) % 4
        d = at(i)
        densify(1 - y, d)
        psend[0, d] = product(0, 1 - y, d)

        @pl.when(i >= 2)
        def _():
            y_copy(0, i).start()

        @pl.when(is_end & (i == 0))
        def _():
            b_copy(0).start()

    @pl.when(is_mid)
    def _():
        r_up.wait_recv()
        w_end_y.start()
        w_half_end.start()
        r_own_y.wait_recv()
        w_half.start()
        w_mids.start()

    f_mate.wait_recv()

    @pl.loop(0, 4)
    def _(step):
        i = (4 - (z + 1) % 4 // 2 - step) % 4
        d = at(i)
        psend[1, d] = product(1, 1 - y, d)

        @pl.when(i >= 2)
        def _():
            y_copy(1, i).start()

        @pl.when(is_end & (i == 0))
        def _():
            b_copy(1).start()

    @pl.when(is_end)
    def _():
        y_copy(0, 1).start()

    @pl.loop(0, 4)
    def _(step):
        d = at(3 - step)
        densify(y, d)
        own[0, d] = product(0, y, d)
        own[1, d] = product(1, y, d)

    @pl.when(is_end)
    def _():
        add_end(0, 3)
        add_end(0, 2)
        add_end(1, 3)

    @pl.when(is_mid)
    def _():
        merge(0)
        r_half_end.wait_recv()
        w_other_end.start()
        r_half.wait_recv()
        w_other.start()
        merge(1)
        r_end_y.wait_recv()
        w_end.start()
        w_half_last.start()
        add_mid(0, 3)

    f_across.wait_recv()
    f_fwd.start()

    @pl.loop(0, 4)
    def _(step):
        d = at(3 - step)
        psend[2, d] = product(2, 1 - y, d)

        @pl.when(step == 0)
        def _():
            y_copy(2, 3).start()

    @pl.when(is_end)
    def _():
        @pl.when(less)
        def _():
            b_half(0).start()

        add_end(1, 2)

    @pl.when(is_mid)
    def _():
        @pl.when(less)
        def _():
            b_half(128).start()

        @pl.when(jnp.logical_not(less))
        def _():
            b_copy(2).start()

        r_half_last.wait_recv()
        w_other_last.start()
        add_mid(0, 2)

    f_fwd.wait_recv()

    @pl.loop(0, 4)
    def _(step):
        d = at(3 - step)
        psend[3, d] = product(3, 1 - y, d)

        @pl.when(step == 0)
        def _():
            y_copy(3, 3).start()
            y_copy(2, 2).start()

    @pl.when(is_end)
    def _():
        y_copy(3, 2).start()
        y_copy(1, 1).start()
        y_copy(2, 1).start()
        y_copy(3, 1).start()
        add_end(0, 1)

    @pl.when(is_mid)
    def _():
        g_copy.start()
        b_copy(3).start()
        v_across.start()
        v_mate.start()

    @pl.loop(0, 4)
    def _(step):
        d = at(3 - step)
        own[2, d] = product(2, y, d)
        own[3, d] = product(3, y, d)

    @pl.when(is_end)
    def _():
        add_end(2, 3)
        r_mids.wait_recv()
        r_end.wait_recv()
        r_other.wait_recv()
        r_other_end.wait_recv()
        r_other_last.wait_recv()
        v_across.start()
        v_mate.start()
        add_end(3, 3)

        @pl.when(less)
        def _():
            merge_half(128)

        @pl.when(jnp.logical_not(less))
        def _():
            merge(2)

        merge_tail()
        add_end(2, 2)
        add_end(3, 2)
        add_end(1, 1)

    @pl.when(is_mid)
    def _():
        add_mid(1, 3)

        @pl.when(less)
        def _():
            merge_half(0)

        y_copy(0, 1).start()
        y_copy(1, 1).start()
        y_copy(2, 1).start()
        g_copy.wait_recv()
        psend[3, at(1)] = total([psend.at[3, at(1)], mb])
        y_copy(3, 1).start()
        add_out(0)
        add_mid(1, 2)
        add_mid(2, 3)
        add_mid(3, 3)
        add_mid(2, 2)

    v_across.wait_recv()
    v_fwd.start()

    @pl.when(is_end)
    def _():
        add_end(2, 1)

    @pl.when(is_mid)
    def _():
        add_out(1)
        add_mid(3, 2)
        add_out(2)

    @pl.when(is_end)
    def _():
        add_end(3, 1)

    @pl.when(is_mid)
    def _():
        add_out(3)

    v_mate.wait_recv()
    v_fwd.wait_recv()
    finish(0)
    finish(1)
    finish(2)
    finish_last()

    for copy in (f_mate, f_across, f_fwd, v_mate, v_across, v_fwd):
        copy.wait_send()

    @pl.loop(0, 4)
    def _(k):
        for i in (1, 3):
            y_copy(k, i).wait_send()

    @pl.loop(0, 3)
    def _(k):
        y_copy(k, 2).wait_send()

    @pl.when(is_end)
    def _():
        w_up.wait_send()
        y_copy(3, 2).wait_send()
        for k in (0, 1):
            b_copy(k).wait_send()

        @pl.when(less)
        def _():
            b_half(0).wait_send()
            y_half(128).wait_send()

        @pl.when(jnp.logical_not(less))
        def _():
            y_copy(2, 0).wait_send()

        @pl.loop(0, 4)
        def _(k):
            for i in (2, 3):
                p_copy(k, i).wait_send()

        @pl.loop(0, 3)
        def _(k):
            p_copy(k, 1).wait_send()

        for lo in (0, 128):
            p_tail(lo).wait_send()
            y_tail(lo).wait_send()

    @pl.when(is_mid)
    def _():
        for copy in (w_own_y, w_end_y, w_mids, w_end, w_half, w_half_end, w_half_last, w_other, w_other_end,
                     w_other_last, g_copy):
            copy.wait_send()
        y_copy(0, 0).wait_send()
        y_copy(1, 0).wait_send()
        b_copy(3).wait_send()

        @pl.when(less)
        def _():
            b_half(128).wait_send()
            y_half(0).wait_send()

        @pl.when(jnp.logical_not(less))
        def _():
            b_copy(2).wait_send()

        @pl.loop(0, 4)
        def _(k):
            p_copy(k, 0).wait_send()
            m_copy(k, 3).wait_send()
            m_copy(k, 2).wait_send()


def fused_shards(adjacency_tiles, tile_rows, tile_cols, tile_counts, features, weight):
    tiles = adjacency_tiles[0, 0]
    slots, tb = tiles.shape[:2]
    width = features.shape[1]
    wide = weight.shape[1]
    bf = jnp.bfloat16
    dma = pltpu.SemaphoreType.DMA
    blocks = (4, 4, 256, width)
    return pl.pallas_call(
        layer_kernel,
        out_shape=jax.ShapeDtypeStruct((256, wide), bf),
        in_specs=[pl.BlockSpec(memory_space=pltpu.SMEM)]
        + [pl.BlockSpec(memory_space=pltpu.HBM)] * 5,
        out_specs=pl.BlockSpec(memory_space=pltpu.VMEM),
        scratch_shapes=[
            pltpu.VMEM((2, 1, slots), jnp.int32),
            pltpu.VMEM((1, 128), jnp.int32),
            pltpu.SMEM((1, 128), jnp.int32),
            pltpu.VMEM((slots + 1, tb, tb), bf),
            pltpu.VMEM((2, 4, 256, 1024), bf),
            pltpu.VMEM((4, 1024, width), bf),
            pltpu.VMEM((8, 4, weight.shape[0] // 4, wide), bf),
            pltpu.VMEM(blocks, bf),
            pltpu.VMEM(blocks, bf),
            pltpu.VMEM(blocks, bf),
            pltpu.VMEM(blocks, bf),
            pltpu.VMEM(blocks, bf),
            pltpu.VMEM((4, 256, width), bf),
            pltpu.VMEM((256, width), bf),
            pltpu.VMEM((256, width), jnp.float32),
            pltpu.VMEM((256, width), bf),
            pltpu.VMEM((256, wide), jnp.float32),
            dma((6,)),
            dma((3,)), dma((3,)),
            dma((11,)), dma((11,)),
            dma((3,)), dma((3,)),
            dma((4, 4)), dma((4, 4)),
            dma((4, 4)), dma((4, 4)),
            dma((4, 4)), dma((4, 4)),
            dma((4,)), dma((4,)),
            dma((2,)),
            dma((4,)), dma((4,)),
        ],
        compiler_params=pltpu.CompilerParams(
            collective_id=0, has_side_effects=True, vmem_limit_bytes=48 * 2**20),
    )(tile_counts, *(pltpu.with_memory_space_constraint(a, pltpu.HBM)
                     for a in (tile_rows[0], tile_cols[0], tiles, features, weight)))


def solution(mesh):
    fits = mesh.shape["row"] == 4 and mesh.shape["col"] == 8
    return jax.shard_map(
        fused_shards if fits else shards,
        mesh=mesh,
        in_specs=(
            P("row", "col", None, None, None),
            P("row", "col", None),
            P("row", "col", None),
            P("row", "col"),
            P("col", "row"),
            P("col", None),
        ),
        out_specs=P(("row", "col"), None),
        check_vma=False,
    )
```

```python
import functools

import jax
import jax.numpy as jnp
from jax import lax
from jax.experimental import pallas as pl
from jax.experimental.pallas import tpu as pltpu
from jax.sharding import PartitionSpec as P

MESH = pl.DeviceIdType.MESH


def densify(adjacency_tiles, tile_rows, tile_cols, tile_count, row_blocks, column_blocks):
    slots = adjacency_tiles.shape[0]
    tile_edge = adjacency_tiles.shape[1]
    live_mask = (jnp.arange(slots, dtype=jnp.int32) < tile_count).astype(jnp.bfloat16)
    masked = adjacency_tiles * live_mask[:, None, None]
    grid = jnp.zeros((row_blocks, column_blocks, tile_edge, tile_edge), jnp.bfloat16)
    grid = grid.at[tile_rows, tile_cols].add(masked)
    return grid.transpose(0, 2, 1, 3).reshape(row_blocks * tile_edge, column_blocks * tile_edge)


def reduce_whole(partial_rows):
    return lax.psum_scatter(
        partial_rows.astype(jnp.bfloat16), "col", scatter_dimension=0, tiled=True
    ).astype(jnp.float32)


def shards(adjacency_tiles, tile_rows, tile_cols, tile_counts, features, weight):
    local_tiles = adjacency_tiles[0, 0]
    local_rows = tile_rows[0, 0]
    local_cols = tile_cols[0, 0]
    local_count = tile_counts[0, 0]
    tile_edge = local_tiles.shape[1]
    column_blocks = features.shape[0] // tile_edge
    row_blocks = column_blocks * lax.axis_size("col") // lax.axis_size("row")
    dense_block = densify(
        local_tiles, local_rows, local_cols, local_count, row_blocks, column_blocks
    )
    whole = lax.all_gather(features, "row", axis=1, tiled=True)
    partial_value = jnp.dot(dense_block, whole, preferred_element_type=jnp.float32)
    summed = reduce_whole(partial_value.astype(jnp.bfloat16).astype(jnp.float32))
    aggregated = summed.astype(jnp.bfloat16)
    full_weight = lax.all_gather(weight, "col", axis=0, tiled=True)
    hidden = jnp.dot(aggregated, full_weight, preferred_element_type=jnp.float32)
    return jnp.maximum(hidden, 0.0).astype(jnp.bfloat16)


def layer_kernel(
    count, rows_hbm, cols_hbm, adj_hbm, feat_hbm, w_hbm, out_ref,
    table, inv_lanes, inv, adj, dense, feat, wfull, psend, own, yr, zp, zm, zb, mb, base, acc, hidden,
    lsem, fsend, frecv, wsend, wrecv, vsend, vrecv, ysend, yrecv, psem, prsem, msem, mrsem, bsend, brecv, gsem, tsend, trecv, ready,
):
    p, q = lax.axis_index("row"), lax.axis_index("col")
    y, z = q % 2, q // 2
    mate = p + 1 - 2 * (p % 2)
    across = (p + 2) % 4
    half = z // 2
    pair_z = z + 1 - 2 * (z % 2)
    q_y, q_pair, q_mid = 2 * z + 1 - y, 2 * pair_z + y, 2 * (3 - z) + y
    is_end = z % 3 == 0
    is_mid = z % 3 > 0
    e = 1 - (z + 1) % 4 // 2
    slots = adj_hbm.shape[0]
    tb = adj_hbm.shape[1]
    quarter = wfull.shape[2]

    def at(i):
        return i + half * (3 - 2 * i)

    barrier = pltpu.get_barrier_semaphore()
    neighbours = (
        ({"col": q_y}, y == 0, y == 1),
        ({"row": across}, p // 2 == 0, p // 2 == 1),
        ({"row": mate}, p % 2 == 0, p % 2 == 1),
        ({"col": q_pair}, z % 2 == 0, z % 2 == 1),
        ({"col": q_mid}, z == 1, z == 2),
    )
    for to, later, _ in neighbours:
        @pl.when(later)
        def _():
            pl.semaphore_signal(barrier, inc=1, device_id=to, device_id_type=MESH)

    def wait_ready(n):
        @pl.when(neighbours[n][1])
        def _():
            pl.semaphore_wait(ready.at[n], 1)

    cp_table = [
        pltpu.make_async_copy(ref, table.at[n], lsem.at[3 + n])
        for n, ref in enumerate((rows_hbm, cols_hbm))
    ]
    for copy in cp_table:
        copy.start()
    cp_adj = pltpu.make_async_copy(adj_hbm, adj.at[pl.ds(0, slots)], lsem.at[0])
    cp_adj.start()
    cp_feat = pltpu.make_async_copy(feat_hbm, feat.at[0], lsem.at[1])
    cp_feat.start()
    w_mine = w_hbm.at[pl.ds(pl.multiple_of(p * quarter, quarter), quarter)]
    cp_w = pltpu.make_async_copy(w_mine, wfull.at[q, p], lsem.at[2])
    cp_w.start()

    greetings = y + p // 2 + p % 2 + z % 2 + (z // 2) * (1 - z % 2)

    @pl.when(greetings > 0)
    def _():
        pl.semaphore_wait(barrier, greetings)

    for n, (to, _, earlier) in enumerate(neighbours):
        @pl.when(earlier)
        def _():
            pl.semaphore_signal(ready.at[n], inc=1, device_id=to, device_id_type=MESH)

    def copy_to(src, dst, ssem, rsem, **to):
        return pltpu.make_async_remote_copy(
            src_ref=src, dst_ref=dst, send_sem=ssem, recv_sem=rsem, device_id=to, device_id_type=MESH)

    f_mate = copy_to(feat_hbm, feat.at[1], fsend.at[0], frecv.at[0], row=mate)
    f_across = copy_to(feat_hbm, feat.at[2], fsend.at[1], frecv.at[1], row=across)
    f_fwd = copy_to(feat.at[2], feat.at[3], fsend.at[2], frecv.at[2], row=mate)
    v_mate = copy_to(wfull.at[:, p], wfull.at[:, p], vsend.at[0], vrecv.at[0], row=mate)
    v_across = copy_to(wfull.at[:, p], wfull.at[:, p], vsend.at[1], vrecv.at[1], row=across)
    v_fwd = copy_to(wfull.at[:, across], wfull.at[:, across], vsend.at[2], vrecv.at[2], row=mate)

    def w_copy(n, ref, to):
        return copy_to(ref, ref, wsend.at[n], wrecv.at[n], col=to)

    def w_block(at_q):
        return wfull.at[at_q, p]

    def w_blocks(first, count):
        return wfull.at[pl.ds(first, count), p]

    w_up = copy_to(w_mine, w_block(q), wsend.at[0], wrecv.at[0], col=q_pair)
    w_own_y = copy_to(w_mine, w_block(q), wsend.at[1], wrecv.at[1], col=q_y)
    w_end_y = w_copy(2, w_block(q_pair), q_y)
    w_mids = w_copy(3, w_blocks(2 * z, 2), q_pair)
    w_end = w_copy(4, w_block(2 * pair_z + 1 - y), q_pair)
    w_half = w_copy(5, w_blocks(2 * z, 2), q_mid)
    w_half_end = w_copy(7, w_block(q_pair), q_mid)
    w_half_last = w_copy(8, w_block(2 * pair_z + 1 - y), q_mid)
    w_other = w_copy(6, w_blocks(6 - 2 * z, 2), q_pair)
    w_other_end = w_copy(9, w_block(2 * (3 - pair_z) + y), q_pair)
    w_other_last = w_copy(10, w_block(2 * (3 - pair_z) + 1 - y), q_pair)
    r_up = w_copy(0, w_block(q_pair), q_pair)
    r_own_y = w_copy(1, w_block(q_y), q_y)
    r_end_y = w_copy(2, w_block(2 * pair_z + 1 - y), q_y)
    r_mids = w_copy(3, w_blocks(2 * pair_z, 2), q_pair)
    r_end = w_copy(4, w_block(q_y), q_pair)
    r_half = w_copy(5, w_blocks(6 - 2 * z, 2), q_mid)
    r_half_end = w_copy(7, w_block(2 * (3 - pair_z) + y), q_mid)
    r_half_last = w_copy(8, w_block(2 * (3 - pair_z) + 1 - y), q_mid)
    r_other = w_copy(6, w_blocks(6 - 2 * pair_z, 2), q_pair)
    r_other_end = w_copy(9, w_block(2 * (3 - z) + y), q_pair)
    r_other_last = w_copy(10, w_block(2 * (3 - z) + 1 - y), q_pair)

    def y_copy(k, i):
        d = at(i)
        return copy_to(psend.at[k, d], yr.at[k, d], ysend.at[k, d], yrecv.at[k, d], col=q_y)

    def p_copy(k, i):
        d = at(i)
        return copy_to(own.at[k, d], zp.at[k, d], psem.at[k, d], prsem.at[k, d], col=q_pair)

    def m_copy(k, i):
        d = at(i)
        return copy_to(own.at[k, d], zm.at[k, d], msem.at[k, d], mrsem.at[k, d], col=q_mid)

    def g_copy(k):
        return copy_to(psend.at[k, at(2)], mb.at[k], gsem.at[0, k], gsem.at[1, k], col=q_mid)

    def b_copy(k):
        return copy_to(psend.at[k, at(0)], zb.at[k], bsend.at[k], brecv.at[k], col=q_pair)

    def part(lo):
        return pl.ds(lo, 128)

    def y_tail(lo):
        d = at(0)
        return copy_to(psend.at[3, d, part(lo)], yr.at[3, d, part(lo)], tsend.at[lo // 128], trecv.at[lo // 128], col=q_y)

    def p_tail(lo):
        d = at(1)
        return copy_to(own.at[3, d, part(lo)], zp.at[3, d, part(lo)], tsend.at[2 + lo // 128], trecv.at[2 + lo // 128], col=q_pair)

    def densify(side, d):
        base = (2 * d + side) * 16
        for up in range(2):
            for cb in range(8):
                dense[side, d, up * tb:(up + 1) * tb, cb * tb:(cb + 1) * tb] = adj[inv[0, base + up * 8 + cb]]

    def product(k, side, d):
        return jnp.dot(dense[side, d], feat[k], preferred_element_type=jnp.float32).astype(jnp.bfloat16)

    def total(refs):
        out = refs[0][...].astype(jnp.float32)
        for ref in refs[1:]:
            out = out + ref[...].astype(jnp.float32)
        return out.astype(jnp.bfloat16)

    def add_end(k, i):
        d = at(i)
        y_copy(k, i).wait_recv()
        own[k, d] = total([own.at[k, d], yr.at[k, d]])
        if (k, i) == (3, 1):
            p_tail(0).start()
            p_tail(128).start()
        else:
            p_copy(k, i).start()

    def add_mid(k, i):
        d = at(i)
        p_copy(k, i).wait_recv()
        if k < 2 and i == 2:
            own[k, d] = total([own.at[k, d], zp.at[k, d]])
        else:
            y_copy(k, i).wait_recv()
            own[k, d] = total([own.at[k, d], yr.at[k, d], zp.at[k, d]])
        m_copy(k, i).start()

    def add_out(k):
        d = at(0)
        m_copy(k, 0).wait_recv()
        if k < 2:
            y_copy(k, 0).wait_recv()
            own[k, d] = total([own.at[k, d], yr.at[k, d], zm.at[k, d]])
        else:
            own[k, d] = total([own.at[k, d], zm.at[k, d]])
        p_copy(k, 0).start()

    def gather_mid(k):
        d = at(1)
        g_copy(k).wait_recv()
        psend[k, d] = total([psend.at[k, d], mb.at[k]])
        y_copy(k, 1).start()

    def merge(k):
        d = at(0)
        b_copy(k).wait_recv()
        psend[k, d] = total([psend.at[k, d], zb.at[k]])
        y_copy(k, 0).start()

    def merge_tail():
        d = at(0)
        b_copy(3).wait_recv()
        psend[3, d] = total([psend.at[3, d], zb.at[3]])
        y_tail(0).start()
        y_tail(128).start()

    def settle(k):
        @pl.when(is_end)
        def _():
            p_copy(k, 0).wait_recv()
            if k == 2:
                y_copy(k, 0).wait_recv()
                acc[...] = total([own.at[k, z], zp.at[k, z], yr.at[k, z]])
            else:
                acc[...] = total([own.at[k, z], zp.at[k, z]])

        @pl.when(is_mid)
        def _():
            y_copy(k, 1).wait_recv()
            m_copy(k, 1).wait_recv()
            p_copy(k, 1).wait_recv()
            acc[...] = total([own.at[k, z], yr.at[k, z], zm.at[k, z], zp.at[k, z]])

    panels = (p, mate, across, (mate + 2) % 4)

    def weight_rows(k):
        return wfull[pl.ds(2 * panels[k], 2)].reshape(8 * quarter, wfull.shape[3])

    def finish(k):
        settle(k)
        term = jnp.dot(acc[...], weight_rows(k), preferred_element_type=jnp.float32)
        if k == 0:
            hidden[...] = term
        else:
            hidden[...] += term

    def finish_last():
        @pl.when(is_end)
        def _():
            p_copy(3, 0).wait_recv()
            base[...] = own[3, z].astype(jnp.float32) + zp[3, z].astype(jnp.float32)

        @pl.when(is_mid)
        def _():
            y_copy(3, 1).wait_recv()
            m_copy(3, 1).wait_recv()
            base[...] = (own[3, z].astype(jnp.float32) + yr[3, z].astype(jnp.float32)) + zm[3, z].astype(jnp.float32)

        for lo in (0, 128):
            rows = slice(lo, lo + 128)

            @pl.when(is_end)
            def _():
                y_tail(lo).wait_recv()
                acc[rows] = (base[rows] + yr[3, z, rows].astype(jnp.float32)).astype(jnp.bfloat16)

            @pl.when(is_mid)
            def _():
                p_tail(lo).wait_recv()
                acc[rows] = (base[rows] + zp[3, z, rows].astype(jnp.float32)).astype(jnp.bfloat16)

            term = jnp.dot(acc[rows], weight_rows(3), preferred_element_type=jnp.float32)
            out_ref[rows] = jnp.maximum(hidden[rows] + term, 0.0).astype(jnp.bfloat16)

    @pl.when(z == 3)
    def _():
        w_up.start()

    @pl.when(is_mid & (y == 1))
    def _():
        w_own_y.start()

    adj[slots] = jnp.zeros((tb, tb), jnp.bfloat16)
    for copy in cp_table:
        copy.wait()
    wide = (128, slots)
    slot = lax.broadcasted_iota(jnp.int32, wide, 1)
    key = jnp.broadcast_to(table[0] * 8 + table[1], wide)
    hit = (key == lax.broadcasted_iota(jnp.int32, wide, 0)) & (slot < count[0, 0])
    found = jnp.min(jnp.where(hit, slot, slots), axis=1, keepdims=True)
    square = (128, 128)
    diagonal = lax.broadcasted_iota(jnp.int32, square, 0) == lax.broadcasted_iota(jnp.int32, square, 1)
    inv_lanes[...] = jnp.min(jnp.where(diagonal, found, slots), axis=0, keepdims=True)
    cp_inv = pltpu.make_async_copy(inv_lanes, inv, lsem.at[5])
    cp_inv.start()

    wait_ready(1)
    f_across.start()
    wait_ready(2)
    f_mate.start()
    wait_ready(3)

    @pl.when(z == 0)
    def _():
        w_up.start()

    cp_inv.wait()
    cp_adj.wait()
    cp_feat.wait()
    mid = 1 - e

    def first(i):
        d = at(i)
        densify(1 - y, d)
        psend[0, d] = product(0, 1 - y, d)
        return i

    def send_first(i):
        @pl.when((i == 3) | (is_end & (i == 2)))
        def _():
            y_copy(0, i).start()

        @pl.when(is_mid & (i == 2))
        def _():
            g_copy(0).start()

        @pl.when(is_end & (i == 0))
        def _():
            b_copy(0).start()

    i_first = first(3 * (y + mid - y * mid))
    wait_ready(0)
    wait_ready(4)

    @pl.when(is_mid & (y == 0))
    def _():
        w_own_y.start()

    send_first(i_first)

    @pl.loop(1, 4)
    def _(step):
        send_first(first(4 - mid - step - 3 * (1 - mid) * y * ((3 - step) // 2)))

    cp_w.wait()

    @pl.when(is_mid)
    def _():
        r_up.wait_recv()
        w_end_y.start()
        w_half_end.start()
        r_own_y.wait_recv()
        w_half.start()
        w_mids.start()

    f_mate.wait_recv()

    @pl.loop(0, 4)
    def _(step):
        i = (3 + e - step) % 4
        d = at(i)
        psend[1, d] = product(1, 1 - y, d)

        @pl.when((i == 3) | (is_end & (i == 2)))
        def _():
            y_copy(1, i).start()

        @pl.when(is_mid & (i == 2))
        def _():
            g_copy(1).start()

        @pl.when(is_end & (i == 0))
        def _():
            b_copy(1).start()

    @pl.when(is_end)
    def _():
        y_copy(0, 1).start()

    def make_own(first, last):
        @pl.loop(first, last)
        def _(step):
            d = at(3 - step)
            densify(y, d)
            own[0, d] = product(0, y, d)
            own[1, d] = product(1, y, d)

    @pl.when(is_end)
    def _():
        make_own(0, 1)
        add_end(0, 3)
        make_own(1, 2)
        add_end(0, 2)
        add_end(1, 3)
        make_own(2, 4)

    @pl.when(is_mid)
    def _():
        merge(0)
        r_half_end.wait_recv()
        w_other_end.start()
        r_half.wait_recv()
        w_other.start()
        merge(1)
        make_own(0, 2)
        r_end_y.wait_recv()
        w_end.start()
        w_half_last.start()
        make_own(2, 4)
        add_mid(0, 3)

    f_across.wait_recv()
    f_fwd.start()

    @pl.loop(0, 4)
    def _(step):
        d = at(3 - step)
        psend[2, d] = product(2, 1 - y, d)

        @pl.when(step == 0)
        def _():
            y_copy(2, 3).start()

    @pl.when(is_end)
    def _():
        add_end(1, 2)

    @pl.when(is_mid)
    def _():
        b_copy(2).start()
        r_half_last.wait_recv()
        w_other_last.start()
        add_mid(0, 2)

    f_fwd.wait_recv()

    @pl.loop(0, 4)
    def _(step):
        d = at(3 - step)
        psend[3, d] = product(3, 1 - y, d)

        @pl.when(step == 0)
        def _():
            y_copy(3, 3).start()

    y_copy(2, 2).start()
    y_copy(3, 2).start()

    @pl.when(is_end)
    def _():
        y_copy(1, 1).start()
        y_copy(2, 1).start()
        y_copy(3, 1).start()
        add_end(0, 1)

    @pl.when(is_mid)
    def _():
        b_copy(3).start()
        v_across.start()
        v_mate.start()

    @pl.loop(0, 4)
    def _(step):
        d = at(3 - step)
        own[2, d] = product(2, y, d)
        own[3, d] = product(3, y, d)

    @pl.when(is_end)
    def _():
        add_end(2, 3)
        r_mids.wait_recv()
        r_end.wait_recv()
        r_other.wait_recv()
        r_other_end.wait_recv()
        r_other_last.wait_recv()
        v_across.start()
        v_mate.start()
        add_end(3, 3)
        merge(2)
        merge_tail()
        add_end(2, 2)
        add_end(3, 2)
        add_end(1, 1)

    @pl.when(is_mid)
    def _():
        add_mid(1, 3)
        gather_mid(0)
        gather_mid(1)
        y_copy(2, 1).start()
        y_copy(3, 1).start()
        add_out(0)
        add_mid(1, 2)
        add_mid(2, 3)
        add_mid(3, 3)
        add_mid(2, 2)

    v_across.wait_recv()
    v_fwd.start()

    @pl.when(is_end)
    def _():
        add_end(2, 1)

    @pl.when(is_mid)
    def _():
        add_out(1)
        add_mid(3, 2)
        add_out(2)

    @pl.when(is_end)
    def _():
        add_end(3, 1)

    @pl.when(is_mid)
    def _():
        add_out(3)

    v_mate.wait_recv()
    v_fwd.wait_recv()
    finish(0)
    finish(1)

    for copy in (f_mate, f_across, f_fwd, v_mate, v_across):
        copy.wait_send()

    @pl.loop(0, 2)
    def _(k):
        y_copy(k, 1).wait_send()
        y_copy(k, 3).wait_send()
        b_copy(k + 2 - 2 * e).wait_send()
        y_copy(k + 2, 3).wait_send()
        y_copy(k + 2, 2).wait_send()

    @pl.when(is_end)
    def _():
        w_up.wait_send()

        @pl.loop(0, 2)
        def _(k):
            y_copy(k, 2).wait_send()
            for i in (1, 2, 3):
                p_copy(k, i).wait_send()
            p_copy(k + 2, 3).wait_send()

    @pl.when(is_mid)
    def _():
        for copy in (w_own_y, w_end_y, w_mids, w_end, w_half, w_half_end, w_half_last, w_other, w_other_end,
                     w_other_last):
            copy.wait_send()

        @pl.loop(0, 2)
        def _(k):
            y_copy(k, 0).wait_send()
            g_copy(k).wait_send()
            p_copy(k, 0).wait_send()
            m_copy(k, 2).wait_send()
            m_copy(k, 3).wait_send()
            m_copy(k + 2, 3).wait_send()

    finish(2)
    finish_last()
    v_fwd.wait_send()
    y_copy(2, 1).wait_send()
    y_copy(3, 1).wait_send()

    @pl.when(is_end)
    def _():
        y_copy(2, 0).wait_send()
        p_copy(2, 2).wait_send()
        p_copy(3, 2).wait_send()
        p_copy(2, 1).wait_send()
        for lo in (0, 128):
            p_tail(lo).wait_send()
            y_tail(lo).wait_send()

    @pl.when(is_mid)
    def _():
        for k in (2, 3):
            m_copy(k, 2).wait_send()
            p_copy(k, 0).wait_send()


def fused_shards(adjacency_tiles, tile_rows, tile_cols, tile_counts, features, weight):
    tiles = adjacency_tiles[0, 0]
    slots, tb = tiles.shape[:2]
    width = features.shape[1]
    wide = weight.shape[1]
    bf = jnp.bfloat16
    dma = pltpu.SemaphoreType.DMA
    blocks = (4, 4, 256, width)
    return pl.pallas_call(
        layer_kernel,
        out_shape=jax.ShapeDtypeStruct((256, wide), bf),
        in_specs=[pl.BlockSpec(memory_space=pltpu.SMEM)]
        + [pl.BlockSpec(memory_space=pltpu.HBM)] * 5,
        out_specs=pl.BlockSpec(memory_space=pltpu.VMEM),
        scratch_shapes=[
            pltpu.VMEM((2, 1, slots), jnp.int32),
            pltpu.VMEM((1, 128), jnp.int32),
            pltpu.SMEM((1, 128), jnp.int32),
            pltpu.VMEM((slots + 1, tb, tb), bf),
            pltpu.VMEM((2, 4, 256, 1024), bf),
            pltpu.VMEM((4, 1024, width), bf),
            pltpu.VMEM((8, 4, weight.shape[0] // 4, wide), bf),
            pltpu.VMEM(blocks, bf),
            pltpu.VMEM(blocks, bf),
            pltpu.VMEM(blocks, bf),
            pltpu.VMEM(blocks, bf),
            pltpu.VMEM(blocks, bf),
            pltpu.VMEM((4, 256, width), bf),
            pltpu.VMEM((2, 256, width), bf),
            pltpu.VMEM((256, width), jnp.float32),
            pltpu.VMEM((256, width), bf),
            pltpu.VMEM((256, wide), jnp.float32),
            dma((6,)),
            dma((3,)), dma((3,)),
            dma((11,)), dma((11,)),
            dma((3,)), dma((3,)),
            dma((4, 4)), dma((4, 4)),
            dma((4, 4)), dma((4, 4)),
            dma((4, 4)), dma((4, 4)),
            dma((4,)), dma((4,)),
            dma((2, 2)),
            dma((4,)), dma((4,)),
            pltpu.SemaphoreType.REGULAR((5,)),
        ],
        compiler_params=pltpu.CompilerParams(
            collective_id=0, has_side_effects=True, vmem_limit_bytes=48 * 2**20),
    )(tile_counts, *(pltpu.with_memory_space_constraint(a, pltpu.HBM)
                     for a in (tile_rows[0], tile_cols[0], tiles, features, weight)))


def solution(mesh):
    fits = mesh.shape["row"] == 4 and mesh.shape["col"] == 8
    return jax.shard_map(
        fused_shards if fits else shards,
        mesh=mesh,
        in_specs=(
            P("row", "col", None, None, None),
            P("row", "col", None),
            P("row", "col", None),
            P("row", "col"),
            P("col", "row"),
            P("col", None),
        ),
        out_specs=P(("row", "col"), None),
        check_vma=False,
    )
```

```python
import functools

import jax
import jax.numpy as jnp
from jax import lax
from jax.experimental import pallas as pl
from jax.experimental.pallas import tpu as pltpu
from jax.sharding import PartitionSpec as P

MESH = pl.DeviceIdType.MESH


def densify(adjacency_tiles, tile_rows, tile_cols, tile_count, row_blocks, column_blocks):
    slots = adjacency_tiles.shape[0]
    tile_edge = adjacency_tiles.shape[1]
    live_mask = (jnp.arange(slots, dtype=jnp.int32) < tile_count).astype(jnp.bfloat16)
    masked = adjacency_tiles * live_mask[:, None, None]
    grid = jnp.zeros((row_blocks, column_blocks, tile_edge, tile_edge), jnp.bfloat16)
    grid = grid.at[tile_rows, tile_cols].add(masked)
    return grid.transpose(0, 2, 1, 3).reshape(row_blocks * tile_edge, column_blocks * tile_edge)


def reduce_whole(partial_rows):
    return lax.psum_scatter(
        partial_rows.astype(jnp.bfloat16), "col", scatter_dimension=0, tiled=True
    ).astype(jnp.float32)


def shards(adjacency_tiles, tile_rows, tile_cols, tile_counts, features, weight):
    local_tiles = adjacency_tiles[0, 0]
    local_rows = tile_rows[0, 0]
    local_cols = tile_cols[0, 0]
    local_count = tile_counts[0, 0]
    tile_edge = local_tiles.shape[1]
    column_blocks = features.shape[0] // tile_edge
    row_blocks = column_blocks * lax.axis_size("col") // lax.axis_size("row")
    dense_block = densify(
        local_tiles, local_rows, local_cols, local_count, row_blocks, column_blocks
    )
    whole = lax.all_gather(features, "row", axis=1, tiled=True)
    partial_value = jnp.dot(dense_block, whole, preferred_element_type=jnp.float32)
    summed = reduce_whole(partial_value.astype(jnp.bfloat16).astype(jnp.float32))
    aggregated = summed.astype(jnp.bfloat16)
    full_weight = lax.all_gather(weight, "col", axis=0, tiled=True)
    hidden = jnp.dot(aggregated, full_weight, preferred_element_type=jnp.float32)
    return jnp.maximum(hidden, 0.0).astype(jnp.bfloat16)


def layer_kernel(
    count, rows_hbm, cols_hbm, adj_hbm, feat_hbm, w_hbm, out_ref,
    table, inv_lanes, inv, adj, dense, feat, wfull, psend, own, yr, zp, zm, zb, mb, base, acc, hidden,
    lsem, fsend, frecv, wsend, wrecv, vsend, vrecv, ysend, yrecv, psem, prsem, msem, mrsem, bsend, brecv, gsem, tsend, trecv, ready,
):
    p, q = lax.axis_index("row"), lax.axis_index("col")
    y, z = q % 2, q // 2
    mate = p + 1 - 2 * (p % 2)
    across = (p + 2) % 4
    half = z // 2
    pair_z = z + 1 - 2 * (z % 2)
    q_y, q_pair, q_mid = 2 * z + 1 - y, 2 * pair_z + y, 2 * (3 - z) + y
    is_end = z % 3 == 0
    is_mid = z % 3 > 0
    e = 1 - (z + 1) % 4 // 2
    slots = adj_hbm.shape[0]
    tb = adj_hbm.shape[1]
    quarter = wfull.shape[2]

    def at(i):
        return i + half * (3 - 2 * i)

    barrier = pltpu.get_barrier_semaphore()
    neighbours = (
        ({"col": q_y}, y == 0, y == 1),
        ({"row": across}, p // 2 == 0, p // 2 == 1),
        ({"row": mate}, p % 2 == 0, p % 2 == 1),
        ({"col": q_pair}, z % 2 == 0, z % 2 == 1),
        ({"col": q_mid}, z == 1, z == 2),
    )
    for to, later, _ in neighbours:
        @pl.when(later)
        def _():
            pl.semaphore_signal(barrier, inc=1, device_id=to, device_id_type=MESH)

    def wait_ready(n):
        @pl.when(neighbours[n][1])
        def _():
            pl.semaphore_wait(ready.at[n], 1)

    cp_table = [
        pltpu.make_async_copy(ref, table.at[n], lsem.at[3 + n])
        for n, ref in enumerate((rows_hbm, cols_hbm))
    ]
    for copy in cp_table:
        copy.start()
    cp_adj = pltpu.make_async_copy(adj_hbm, adj.at[pl.ds(0, slots)], lsem.at[0])
    cp_adj.start()
    cp_feat = pltpu.make_async_copy(feat_hbm, feat.at[0], lsem.at[1])
    cp_feat.start()
    w_mine = w_hbm.at[pl.ds(pl.multiple_of(p * quarter, quarter), quarter)]
    cp_w = pltpu.make_async_copy(w_mine, wfull.at[q, p], lsem.at[2])
    cp_w.start()

    greetings = y + p // 2 + p % 2 + z % 2 + (z // 2) * (1 - z % 2)

    @pl.when(greetings > 0)
    def _():
        pl.semaphore_wait(barrier, greetings)

    for n, (to, _, earlier) in enumerate(neighbours):
        @pl.when(earlier)
        def _():
            pl.semaphore_signal(ready.at[n], inc=1, device_id=to, device_id_type=MESH)

    def copy_to(src, dst, ssem, rsem, **to):
        return pltpu.make_async_remote_copy(
            src_ref=src, dst_ref=dst, send_sem=ssem, recv_sem=rsem, device_id=to, device_id_type=MESH)

    f_mate = copy_to(feat_hbm, feat.at[1], fsend.at[0], frecv.at[0], row=mate)
    f_across = copy_to(feat_hbm, feat.at[2], fsend.at[1], frecv.at[1], row=across)
    f_fwd = copy_to(feat.at[2], feat.at[3], fsend.at[2], frecv.at[2], row=mate)
    v_mate = copy_to(wfull.at[:, p], wfull.at[:, p], vsend.at[0], vrecv.at[0], row=mate)
    v_across = copy_to(wfull.at[:, p], wfull.at[:, p], vsend.at[1], vrecv.at[1], row=across)
    v_fwd = copy_to(wfull.at[:, across], wfull.at[:, across], vsend.at[2], vrecv.at[2], row=mate)

    def w_copy(n, ref, to):
        return copy_to(ref, ref, wsend.at[n], wrecv.at[n], col=to)

    def w_block(at_q):
        return wfull.at[at_q, p]

    def w_blocks(first, count):
        return wfull.at[pl.ds(first, count), p]

    w_up = copy_to(w_mine, w_block(q), wsend.at[0], wrecv.at[0], col=q_pair)
    w_own_y = copy_to(w_mine, w_block(q), wsend.at[1], wrecv.at[1], col=q_y)
    w_end_y = w_copy(2, w_block(q_pair), q_y)
    w_mids = w_copy(3, w_blocks(2 * z, 2), q_pair)
    w_end = w_copy(4, w_block(2 * pair_z + 1 - y), q_pair)
    w_half = w_copy(5, w_blocks(2 * z, 2), q_mid)
    w_half_end = w_copy(7, w_block(q_pair), q_mid)
    w_half_last = w_copy(8, w_block(2 * pair_z + 1 - y), q_mid)
    w_other = w_copy(6, w_blocks(6 - 2 * z, 2), q_pair)
    w_other_end = w_copy(9, w_block(2 * (3 - pair_z) + y), q_pair)
    w_other_last = w_copy(10, w_block(2 * (3 - pair_z) + 1 - y), q_pair)
    r_up = w_copy(0, w_block(q_pair), q_pair)
    r_own_y = w_copy(1, w_block(q_y), q_y)
    r_end_y = w_copy(2, w_block(2 * pair_z + 1 - y), q_y)
    r_mids = w_copy(3, w_blocks(2 * pair_z, 2), q_pair)
    r_end = w_copy(4, w_block(q_y), q_pair)
    r_half = w_copy(5, w_blocks(6 - 2 * z, 2), q_mid)
    r_half_end = w_copy(7, w_block(2 * (3 - pair_z) + y), q_mid)
    r_half_last = w_copy(8, w_block(2 * (3 - pair_z) + 1 - y), q_mid)
    r_other = w_copy(6, w_blocks(6 - 2 * pair_z, 2), q_pair)
    r_other_end = w_copy(9, w_block(2 * (3 - z) + y), q_pair)
    r_other_last = w_copy(10, w_block(2 * (3 - z) + 1 - y), q_pair)

    def y_copy(k, i):
        d = at(i)
        return copy_to(psend.at[k, d], yr.at[k, d], ysend.at[k, d], yrecv.at[k, d], col=q_y)

    def p_copy(k, i):
        d = at(i)
        return copy_to(own.at[k, d], zp.at[k, d], psem.at[k, d], prsem.at[k, d], col=q_pair)

    def m_copy(k, i):
        d = at(i)
        return copy_to(own.at[k, d], zm.at[k, d], msem.at[k, d], mrsem.at[k, d], col=q_mid)

    def g_copy(k):
        return copy_to(psend.at[k, at(2)], mb.at[k], gsem.at[0, k], gsem.at[1, k], col=q_mid)

    def b_copy(k):
        return copy_to(psend.at[k, at(0)], zb.at[k], bsend.at[k], brecv.at[k], col=q_pair)

    cut = 192

    def part(lo):
        return pl.ds(lo, 256 - cut if lo else cut)

    def y_tail(lo):
        d = at(0)
        return copy_to(psend.at[3, d, part(lo)], yr.at[3, d, part(lo)], tsend.at[lo // cut], trecv.at[lo // cut], col=q_y)

    def p_tail(lo):
        d = at(1)
        return copy_to(own.at[3, d, part(lo)], zp.at[3, d, part(lo)], tsend.at[2 + lo // cut], trecv.at[2 + lo // cut], col=q_pair)

    def densify(side, d):
        base = (2 * d + side) * 16
        for up in range(2):
            for cb in range(8):
                dense[side, d, up * tb:(up + 1) * tb, cb * tb:(cb + 1) * tb] = adj[inv[0, base + up * 8 + cb]]

    def product(k, side, d):
        return jnp.dot(dense[side, d], feat[k], preferred_element_type=jnp.float32).astype(jnp.bfloat16)

    def total(refs):
        out = refs[0][...].astype(jnp.float32)
        for ref in refs[1:]:
            out = out + ref[...].astype(jnp.float32)
        return out.astype(jnp.bfloat16)

    def add_end(k, i):
        d = at(i)
        y_copy(k, i).wait_recv()
        own[k, d] = total([own.at[k, d], yr.at[k, d]])
        if (k, i) == (3, 1):
            p_tail(0).start()
            p_tail(cut).start()
        else:
            p_copy(k, i).start()

    def add_mid(k, i):
        d = at(i)
        p_copy(k, i).wait_recv()
        if k < 2 and i == 2:
            own[k, d] = total([own.at[k, d], zp.at[k, d]])
        else:
            y_copy(k, i).wait_recv()
            own[k, d] = total([own.at[k, d], yr.at[k, d], zp.at[k, d]])
        m_copy(k, i).start()

    def add_out(k):
        d = at(0)
        m_copy(k, 0).wait_recv()
        if k < 2:
            y_copy(k, 0).wait_recv()
            own[k, d] = total([own.at[k, d], yr.at[k, d], zm.at[k, d]])
        else:
            own[k, d] = total([own.at[k, d], zm.at[k, d]])
        p_copy(k, 0).start()

    def gather_mid(k):
        d = at(1)
        g_copy(k).wait_recv()
        psend[k, d] = total([psend.at[k, d], mb.at[k]])
        y_copy(k, 1).start()

    def merge(k):
        d = at(0)
        b_copy(k).wait_recv()
        psend[k, d] = total([psend.at[k, d], zb.at[k]])
        y_copy(k, 0).start()

    def merge_tail():
        d = at(0)
        b_copy(3).wait_recv()
        psend[3, d] = total([psend.at[3, d], zb.at[3]])
        y_tail(0).start()
        y_tail(cut).start()

    def settle(k):
        @pl.when(is_end)
        def _():
            p_copy(k, 0).wait_recv()
            if k == 2:
                y_copy(k, 0).wait_recv()
                acc[...] = total([own.at[k, z], zp.at[k, z], yr.at[k, z]])
            else:
                acc[...] = total([own.at[k, z], zp.at[k, z]])

        @pl.when(is_mid)
        def _():
            y_copy(k, 1).wait_recv()
            m_copy(k, 1).wait_recv()
            p_copy(k, 1).wait_recv()
            acc[...] = total([own.at[k, z], yr.at[k, z], zm.at[k, z], zp.at[k, z]])

    panels = (p, mate, across, (mate + 2) % 4)

    def weight_rows(k):
        return wfull[pl.ds(2 * panels[k], 2)].reshape(8 * quarter, wfull.shape[3])

    def finish(k):
        settle(k)
        term = jnp.dot(acc[...], weight_rows(k), preferred_element_type=jnp.float32)
        if k == 0:
            hidden[...] = term
        else:
            hidden[...] += term

    def finish_last():
        @pl.when(is_end)
        def _():
            p_copy(3, 0).wait_recv()
            base[...] = own[3, z].astype(jnp.float32) + zp[3, z].astype(jnp.float32)

        @pl.when(is_mid)
        def _():
            y_copy(3, 1).wait_recv()
            m_copy(3, 1).wait_recv()
            base[...] = (own[3, z].astype(jnp.float32) + yr[3, z].astype(jnp.float32)) + zm[3, z].astype(jnp.float32)

        for lo in (0, cut):
            rows = slice(lo, 256 if lo else cut)

            @pl.when(is_end)
            def _():
                y_tail(lo).wait_recv()
                acc[rows] = (base[rows] + yr[3, z, rows].astype(jnp.float32)).astype(jnp.bfloat16)

            @pl.when(is_mid)
            def _():
                p_tail(lo).wait_recv()
                acc[rows] = (base[rows] + zp[3, z, rows].astype(jnp.float32)).astype(jnp.bfloat16)

            term = jnp.dot(acc[rows], weight_rows(3), preferred_element_type=jnp.float32)
            out_ref[rows] = jnp.maximum(hidden[rows] + term, 0.0).astype(jnp.bfloat16)

    @pl.when(z == 3)
    def _():
        w_up.start()

    @pl.when(is_mid & (y == 1))
    def _():
        w_own_y.start()

    adj[slots] = jnp.zeros((tb, tb), jnp.bfloat16)
    for copy in cp_table:
        copy.wait()
    wide = (128, slots)
    slot = lax.broadcasted_iota(jnp.int32, wide, 1)
    key = jnp.broadcast_to(table[0] * 8 + table[1], wide)
    hit = (key == lax.broadcasted_iota(jnp.int32, wide, 0)) & (slot < count[0, 0])
    found = jnp.min(jnp.where(hit, slot, slots), axis=1, keepdims=True)
    square = (128, 128)
    diagonal = lax.broadcasted_iota(jnp.int32, square, 0) == lax.broadcasted_iota(jnp.int32, square, 1)
    inv_lanes[...] = jnp.min(jnp.where(diagonal, found, slots), axis=0, keepdims=True)
    cp_inv = pltpu.make_async_copy(inv_lanes, inv, lsem.at[5])
    cp_inv.start()

    wait_ready(1)
    f_across.start()
    wait_ready(2)
    f_mate.start()
    wait_ready(3)

    @pl.when(z == 0)
    def _():
        w_up.start()

    cp_inv.wait()
    cp_adj.wait()
    cp_feat.wait()
    mid = 1 - e

    def first(i):
        d = at(i)
        densify(1 - y, d)
        psend[0, d] = product(0, 1 - y, d)
        return i

    def send_first(i):
        @pl.when((i == 3) | (is_end & (i == 2)))
        def _():
            y_copy(0, i).start()

        @pl.when(is_mid & (i == 2))
        def _():
            g_copy(0).start()

        @pl.when(is_end & (i == 0))
        def _():
            b_copy(0).start()

    i_first = first(3 * (y + mid - y * mid))
    wait_ready(0)
    wait_ready(4)

    @pl.when(is_mid & (y == 0))
    def _():
        w_own_y.start()

    send_first(i_first)

    @pl.loop(1, 4)
    def _(step):
        send_first(first(4 - mid - step - 3 * (1 - mid) * y * ((3 - step) // 2)))

    cp_w.wait()

    @pl.when(is_mid)
    def _():
        r_up.wait_recv()
        w_end_y.start()
        w_half_end.start()
        r_own_y.wait_recv()
        w_half.start()
        w_mids.start()

    f_mate.wait_recv()

    @pl.loop(0, 4)
    def _(step):
        i = (3 + e - step) % 4
        d = at(i)
        psend[1, d] = product(1, 1 - y, d)

        @pl.when((i == 3) | (is_end & (i == 2)))
        def _():
            y_copy(1, i).start()

        @pl.when(is_mid & (i == 2))
        def _():
            g_copy(1).start()

        @pl.when(is_end & (i == 0))
        def _():
            b_copy(1).start()

    @pl.when(is_end)
    def _():
        y_copy(0, 1).start()

    def make_own(first, last):
        @pl.loop(first, last)
        def _(step):
            d = at(3 - step)
            densify(y, d)
            own[0, d] = product(0, y, d)
            own[1, d] = product(1, y, d)

    @pl.when(is_end)
    def _():
        make_own(0, 1)
        add_end(0, 3)
        make_own(1, 2)
        add_end(0, 2)
        add_end(1, 3)
        make_own(2, 4)

    @pl.when(is_mid)
    def _():
        merge(0)
        r_half_end.wait_recv()
        w_other_end.start()
        r_half.wait_recv()
        w_other.start()
        merge(1)
        make_own(0, 2)
        r_end_y.wait_recv()
        w_end.start()
        w_half_last.start()
        make_own(2, 4)
        add_mid(0, 3)

    f_across.wait_recv()
    f_fwd.start()

    @pl.loop(0, 4)
    def _(step):
        d = at(3 - step)
        psend[2, d] = product(2, 1 - y, d)

        @pl.when(step == 0)
        def _():
            y_copy(2, 3).start()

    @pl.when(is_end)
    def _():
        add_end(1, 2)

    @pl.when(is_mid)
    def _():
        b_copy(2).start()
        r_half_last.wait_recv()
        w_other_last.start()
        add_mid(0, 2)

    f_fwd.wait_recv()

    @pl.loop(0, 4)
    def _(step):
        d = at(3 - step)
        psend[3, d] = product(3, 1 - y, d)

        @pl.when(step == 0)
        def _():
            y_copy(3, 3).start()

    y_copy(2, 2).start()
    y_copy(3, 2).start()

    @pl.when(is_end)
    def _():
        y_copy(1, 1).start()
        y_copy(2, 1).start()
        y_copy(3, 1).start()
        add_end(0, 1)

    @pl.when(is_mid)
    def _():
        b_copy(3).start()
        v_across.start()
        v_mate.start()

    @pl.loop(0, 4)
    def _(step):
        d = at(3 - step)
        own[2, d] = product(2, y, d)
        own[3, d] = product(3, y, d)

    @pl.when(is_end)
    def _():
        add_end(2, 3)
        r_mids.wait_recv()
        r_end.wait_recv()
        r_other.wait_recv()
        r_other_end.wait_recv()
        r_other_last.wait_recv()
        v_across.start()
        v_mate.start()
        add_end(3, 3)
        merge(2)
        merge_tail()
        add_end(2, 2)
        add_end(3, 2)
        add_end(1, 1)

    @pl.when(is_mid)
    def _():
        add_mid(1, 3)
        gather_mid(0)
        gather_mid(1)
        y_copy(2, 1).start()
        y_copy(3, 1).start()
        add_out(0)
        add_mid(1, 2)
        add_mid(2, 3)
        add_mid(3, 3)
        add_mid(2, 2)

    v_across.wait_recv()
    v_fwd.start()

    @pl.when(is_end)
    def _():
        add_end(2, 1)

    @pl.when(is_mid)
    def _():
        add_out(1)
        add_mid(3, 2)
        add_out(2)

    @pl.when(is_end)
    def _():
        add_end(3, 1)

    @pl.when(is_mid)
    def _():
        add_out(3)

    v_mate.wait_recv()
    v_fwd.wait_recv()
    finish(0)
    finish(1)

    for copy in (f_mate, f_across, f_fwd, v_mate, v_across):
        copy.wait_send()

    @pl.loop(0, 2)
    def _(k):
        y_copy(k, 1).wait_send()
        y_copy(k, 3).wait_send()
        b_copy(k + 2 - 2 * e).wait_send()
        y_copy(k + 2, 3).wait_send()
        y_copy(k + 2, 2).wait_send()

    @pl.when(is_end)
    def _():
        w_up.wait_send()

        @pl.loop(0, 2)
        def _(k):
            y_copy(k, 2).wait_send()
            for i in (1, 2, 3):
                p_copy(k, i).wait_send()
            p_copy(k + 2, 3).wait_send()

    @pl.when(is_mid)
    def _():
        for copy in (w_own_y, w_end_y, w_mids, w_end, w_half, w_half_end, w_half_last, w_other, w_other_end,
                     w_other_last):
            copy.wait_send()

        @pl.loop(0, 2)
        def _(k):
            y_copy(k, 0).wait_send()
            g_copy(k).wait_send()
            p_copy(k, 0).wait_send()
            m_copy(k, 2).wait_send()
            m_copy(k, 3).wait_send()
            m_copy(k + 2, 3).wait_send()

    finish(2)
    finish_last()
    v_fwd.wait_send()
    y_copy(2, 1).wait_send()
    y_copy(3, 1).wait_send()

    @pl.when(is_end)
    def _():
        y_copy(2, 0).wait_send()
        p_copy(2, 2).wait_send()
        p_copy(3, 2).wait_send()
        p_copy(2, 1).wait_send()
        for lo in (0, cut):
            p_tail(lo).wait_send()
            y_tail(lo).wait_send()

    @pl.when(is_mid)
    def _():
        for k in (2, 3):
            m_copy(k, 2).wait_send()
            p_copy(k, 0).wait_send()


def fused_shards(adjacency_tiles, tile_rows, tile_cols, tile_counts, features, weight):
    tiles = adjacency_tiles[0, 0]
    slots, tb = tiles.shape[:2]
    width = features.shape[1]
    wide = weight.shape[1]
    bf = jnp.bfloat16
    dma = pltpu.SemaphoreType.DMA
    blocks = (4, 4, 256, width)
    return pl.pallas_call(
        layer_kernel,
        out_shape=jax.ShapeDtypeStruct((256, wide), bf),
        in_specs=[pl.BlockSpec(memory_space=pltpu.SMEM)]
        + [pl.BlockSpec(memory_space=pltpu.HBM)] * 5,
        out_specs=pl.BlockSpec(memory_space=pltpu.VMEM),
        scratch_shapes=[
            pltpu.VMEM((2, 1, slots), jnp.int32),
            pltpu.VMEM((1, 128), jnp.int32),
            pltpu.SMEM((1, 128), jnp.int32),
            pltpu.VMEM((slots + 1, tb, tb), bf),
            pltpu.VMEM((2, 4, 256, 1024), bf),
            pltpu.VMEM((4, 1024, width), bf),
            pltpu.VMEM((8, 4, weight.shape[0] // 4, wide), bf),
            pltpu.VMEM(blocks, bf),
            pltpu.VMEM(blocks, bf),
            pltpu.VMEM(blocks, bf),
            pltpu.VMEM(blocks, bf),
            pltpu.VMEM(blocks, bf),
            pltpu.VMEM((4, 256, width), bf),
            pltpu.VMEM((2, 256, width), bf),
            pltpu.VMEM((256, width), jnp.float32),
            pltpu.VMEM((256, width), bf),
            pltpu.VMEM((256, wide), jnp.float32),
            dma((6,)),
            dma((3,)), dma((3,)),
            dma((11,)), dma((11,)),
            dma((3,)), dma((3,)),
            dma((4, 4)), dma((4, 4)),
            dma((4, 4)), dma((4, 4)),
            dma((4, 4)), dma((4, 4)),
            dma((4,)), dma((4,)),
            dma((2, 2)),
            dma((4,)), dma((4,)),
            pltpu.SemaphoreType.REGULAR((5,)),
        ],
        compiler_params=pltpu.CompilerParams(
            collective_id=0, has_side_effects=True, vmem_limit_bytes=48 * 2**20),
    )(tile_counts, *(pltpu.with_memory_space_constraint(a, pltpu.HBM)
                     for a in (tile_rows[0], tile_cols[0], tiles, features, weight)))


def solution(mesh):
    fits = mesh.shape["row"] == 4 and mesh.shape["col"] == 8
    return jax.shard_map(
        fused_shards if fits else shards,
        mesh=mesh,
        in_specs=(
            P("row", "col", None, None, None),
            P("row", "col", None),
            P("row", "col", None),
            P("row", "col"),
            P("col", "row"),
            P("col", None),
        ),
        out_specs=P(("row", "col"), None),
        check_vma=False,
    )
```

```python
import functools

import jax
import jax.numpy as jnp
from jax import lax
from jax.experimental import pallas as pl
from jax.experimental.pallas import tpu as pltpu
from jax.sharding import PartitionSpec as P

MESH = pl.DeviceIdType.MESH


def densify(adjacency_tiles, tile_rows, tile_cols, tile_count, row_blocks, column_blocks):
    slots = adjacency_tiles.shape[0]
    tile_edge = adjacency_tiles.shape[1]
    live_mask = (jnp.arange(slots, dtype=jnp.int32) < tile_count).astype(jnp.bfloat16)
    masked = adjacency_tiles * live_mask[:, None, None]
    grid = jnp.zeros((row_blocks, column_blocks, tile_edge, tile_edge), jnp.bfloat16)
    grid = grid.at[tile_rows, tile_cols].add(masked)
    return grid.transpose(0, 2, 1, 3).reshape(row_blocks * tile_edge, column_blocks * tile_edge)


def reduce_whole(partial_rows):
    return lax.psum_scatter(
        partial_rows.astype(jnp.bfloat16), "col", scatter_dimension=0, tiled=True
    ).astype(jnp.float32)


def shards(adjacency_tiles, tile_rows, tile_cols, tile_counts, features, weight):
    local_tiles = adjacency_tiles[0, 0]
    local_rows = tile_rows[0, 0]
    local_cols = tile_cols[0, 0]
    local_count = tile_counts[0, 0]
    tile_edge = local_tiles.shape[1]
    column_blocks = features.shape[0] // tile_edge
    row_blocks = column_blocks * lax.axis_size("col") // lax.axis_size("row")
    dense_block = densify(
        local_tiles, local_rows, local_cols, local_count, row_blocks, column_blocks
    )
    whole = lax.all_gather(features, "row", axis=1, tiled=True)
    partial_value = jnp.dot(dense_block, whole, preferred_element_type=jnp.float32)
    summed = reduce_whole(partial_value.astype(jnp.bfloat16).astype(jnp.float32))
    aggregated = summed.astype(jnp.bfloat16)
    full_weight = lax.all_gather(weight, "col", axis=0, tiled=True)
    hidden = jnp.dot(aggregated, full_weight, preferred_element_type=jnp.float32)
    return jnp.maximum(hidden, 0.0).astype(jnp.bfloat16)


def layer_kernel(
    count, rows_hbm, cols_hbm, adj_hbm, feat_hbm, w_hbm, out_ref,
    table, inv_lanes, inv, adj, dense, feat, wfull, psend, own, yr, zp, zm, zb, mb, base, acc, hidden,
    lsem, fsend, frecv, wsend, wrecv, vsend, vrecv, ysend, yrecv, psem, prsem, msem, mrsem, bsend, brecv, gsem, tsend, trecv, ready,
):
    p, q = lax.axis_index("row"), lax.axis_index("col")
    y, z = q % 2, q // 2
    mate = p + 1 - 2 * (p % 2)
    across = (p + 2) % 4
    half = z // 2
    pair_z = z + 1 - 2 * (z % 2)
    q_y, q_pair, q_mid = 2 * z + 1 - y, 2 * pair_z + y, 2 * (3 - z) + y
    is_end = z % 3 == 0
    is_mid = z % 3 > 0
    e = 1 - (z + 1) % 4 // 2
    slots = adj_hbm.shape[0]
    tb = adj_hbm.shape[1]
    quarter = wfull.shape[2]

    def at(i):
        return i + half * (3 - 2 * i)

    barrier = pltpu.get_barrier_semaphore()
    neighbours = (
        ({"col": q_y}, y == 0, y == 1),
        ({"row": across}, p // 2 == 0, p // 2 == 1),
        ({"row": mate}, p % 2 == 0, p % 2 == 1),
        ({"col": q_pair}, z % 2 == 0, z % 2 == 1),
        ({"col": q_mid}, z == 1, z == 2),
    )
    for to, later, _ in neighbours:
        @pl.when(later)
        def _():
            pl.semaphore_signal(barrier, inc=1, device_id=to, device_id_type=MESH)

    def wait_ready(n):
        @pl.when(neighbours[n][1])
        def _():
            pl.semaphore_wait(ready.at[n], 1)

    cp_table = [
        pltpu.make_async_copy(ref, table.at[n], lsem.at[3 + n])
        for n, ref in enumerate((rows_hbm, cols_hbm))
    ]
    for copy in cp_table:
        copy.start()
    cp_adj = pltpu.make_async_copy(adj_hbm, adj.at[pl.ds(0, slots)], lsem.at[0])
    cp_adj.start()
    cp_feat = pltpu.make_async_copy(feat_hbm, feat.at[0], lsem.at[1])
    cp_feat.start()
    w_mine = w_hbm.at[pl.ds(pl.multiple_of(p * quarter, quarter), quarter)]
    cp_w = pltpu.make_async_copy(w_mine, wfull.at[q, p], lsem.at[2])
    cp_w.start()

    greetings = y + p // 2 + p % 2 + z % 2 + (z // 2) * (1 - z % 2)

    @pl.when(greetings > 0)
    def _():
        pl.semaphore_wait(barrier, greetings)

    for n, (to, _, earlier) in enumerate(neighbours):
        @pl.when(earlier)
        def _():
            pl.semaphore_signal(ready.at[n], inc=1, device_id=to, device_id_type=MESH)

    def copy_to(src, dst, ssem, rsem, **to):
        return pltpu.make_async_remote_copy(
            src_ref=src, dst_ref=dst, send_sem=ssem, recv_sem=rsem, device_id=to, device_id_type=MESH)

    f_mate = copy_to(feat_hbm, feat.at[1], fsend.at[0], frecv.at[0], row=mate)
    f_across = copy_to(feat_hbm, feat.at[2], fsend.at[1], frecv.at[1], row=across)
    f_fwd = copy_to(feat.at[2], feat.at[3], fsend.at[2], frecv.at[2], row=mate)
    v_mate = copy_to(wfull.at[:, p], wfull.at[:, p], vsend.at[0], vrecv.at[0], row=mate)
    v_across = copy_to(wfull.at[:, p], wfull.at[:, p], vsend.at[1], vrecv.at[1], row=across)
    v_fwd = copy_to(wfull.at[:, across], wfull.at[:, across], vsend.at[2], vrecv.at[2], row=mate)

    def w_copy(n, ref, to):
        return copy_to(ref, ref, wsend.at[n], wrecv.at[n], col=to)

    def w_block(at_q):
        return wfull.at[at_q, p]

    def w_blocks(first, count):
        return wfull.at[pl.ds(first, count), p]

    w_up = copy_to(w_mine, w_block(q), wsend.at[0], wrecv.at[0], col=q_pair)
    w_own_y = copy_to(w_mine, w_block(q), wsend.at[1], wrecv.at[1], col=q_y)
    w_end_y = w_copy(2, w_block(q_pair), q_y)
    w_mids = w_copy(3, w_blocks(2 * z, 2), q_pair)
    w_end = w_copy(4, w_block(2 * pair_z + 1 - y), q_pair)
    w_half = w_copy(5, w_blocks(2 * z, 2), q_mid)
    w_half_end = w_copy(7, w_block(q_pair), q_mid)
    w_half_last = w_copy(8, w_block(2 * pair_z + 1 - y), q_mid)
    w_other = w_copy(6, w_blocks(6 - 2 * z, 2), q_pair)
    w_other_end = w_copy(9, w_block(2 * (3 - pair_z) + y), q_pair)
    w_other_last = w_copy(10, w_block(2 * (3 - pair_z) + 1 - y), q_pair)
    r_up = w_copy(0, w_block(q_pair), q_pair)
    r_own_y = w_copy(1, w_block(q_y), q_y)
    r_end_y = w_copy(2, w_block(2 * pair_z + 1 - y), q_y)
    r_mids = w_copy(3, w_blocks(2 * pair_z, 2), q_pair)
    r_end = w_copy(4, w_block(q_y), q_pair)
    r_half = w_copy(5, w_blocks(6 - 2 * z, 2), q_mid)
    r_half_end = w_copy(7, w_block(2 * (3 - pair_z) + y), q_mid)
    r_half_last = w_copy(8, w_block(2 * (3 - pair_z) + 1 - y), q_mid)
    r_other = w_copy(6, w_blocks(6 - 2 * pair_z, 2), q_pair)
    r_other_end = w_copy(9, w_block(2 * (3 - z) + y), q_pair)
    r_other_last = w_copy(10, w_block(2 * (3 - z) + 1 - y), q_pair)

    def y_copy(k, i):
        d = at(i)
        return copy_to(psend.at[k, d], yr.at[k, d], ysend.at[k, d], yrecv.at[k, d], col=q_y)

    def p_copy(k, i):
        d = at(i)
        return copy_to(own.at[k, d], zp.at[k, d], psem.at[k, d], prsem.at[k, d], col=q_pair)

    def m_copy(k, i):
        d = at(i)
        return copy_to(own.at[k, d], zm.at[k, d], msem.at[k, d], mrsem.at[k, d], col=q_mid)

    def g_copy(k):
        return copy_to(psend.at[k, at(2)], mb.at[k], gsem.at[0, k], gsem.at[1, k], col=q_mid)

    def b_copy(k):
        return copy_to(psend.at[k, at(0)], zb.at[k], bsend.at[k], brecv.at[k], col=q_pair)

    def part(lo):
        return pl.ds(lo, 128)

    def y_tail(lo):
        d = at(0)
        return copy_to(psend.at[3, d, part(lo)], yr.at[3, d, part(lo)], tsend.at[lo // 128], trecv.at[lo // 128], col=q_y)

    def p_tail(lo):
        d = at(1)
        return copy_to(own.at[3, d, part(lo)], zp.at[3, d, part(lo)], tsend.at[2 + lo // 128], trecv.at[2 + lo // 128], col=q_pair)

    def densify(side, d):
        base = (2 * d + side) * 16
        for up in range(2):
            for cb in range(8):
                dense[side, d, up * tb:(up + 1) * tb, cb * tb:(cb + 1) * tb] = adj[inv[0, base + up * 8 + cb]]

    def product(k, side, d):
        return jnp.dot(dense[side, d], feat[k], preferred_element_type=jnp.float32).astype(jnp.bfloat16)

    def total(refs):
        out = refs[0][...].astype(jnp.float32)
        for ref in refs[1:]:
            out = out + ref[...].astype(jnp.float32)
        return out.astype(jnp.bfloat16)

    def add_end(k, i):
        d = at(i)
        y_copy(k, i).wait_recv()
        own[k, d] = total([own.at[k, d], yr.at[k, d]])
        if (k, i) == (3, 1):
            p_tail(0).start()
            p_tail(128).start()
        else:
            p_copy(k, i).start()

    def add_mid(k, i):
        d = at(i)
        p_copy(k, i).wait_recv()
        if k < 2 and i == 2:
            own[k, d] = total([own.at[k, d], zp.at[k, d]])
        else:
            y_copy(k, i).wait_recv()
            own[k, d] = total([own.at[k, d], yr.at[k, d], zp.at[k, d]])
        m_copy(k, i).start()

    def add_out(k):
        d = at(0)
        m_copy(k, 0).wait_recv()
        if k < 2:
            y_copy(k, 0).wait_recv()
            own[k, d] = total([own.at[k, d], yr.at[k, d], zm.at[k, d]])
        else:
            own[k, d] = total([own.at[k, d], zm.at[k, d]])
        p_copy(k, 0).start()

    def gather_mid(k):
        d = at(1)
        g_copy(k).wait_recv()
        psend[k, d] = total([psend.at[k, d], mb.at[k]])
        y_copy(k, 1).start()

    def merge(k):
        d = at(0)
        b_copy(k).wait_recv()
        psend[k, d] = total([psend.at[k, d], zb.at[k]])
        y_copy(k, 0).start()

    def merge_tail():
        d = at(0)
        b_copy(3).wait_recv()
        psend[3, d] = total([psend.at[3, d], zb.at[3]])
        y_tail(0).start()
        y_tail(128).start()

    def settle(k):
        @pl.when(is_end)
        def _():
            p_copy(k, 0).wait_recv()
            if k == 2:
                y_copy(k, 0).wait_recv()
                acc[...] = total([own.at[k, z], zp.at[k, z], yr.at[k, z]])
            else:
                acc[...] = total([own.at[k, z], zp.at[k, z]])

        @pl.when(is_mid)
        def _():
            y_copy(k, 1).wait_recv()
            m_copy(k, 1).wait_recv()
            p_copy(k, 1).wait_recv()
            acc[...] = total([own.at[k, z], yr.at[k, z], zm.at[k, z], zp.at[k, z]])

    panels = (p, mate, across, (mate + 2) % 4)

    def weight_rows(k):
        return wfull[pl.ds(2 * panels[k], 2)].reshape(8 * quarter, wfull.shape[3])

    def finish(k):
        settle(k)
        term = jnp.dot(acc[...], weight_rows(k), preferred_element_type=jnp.float32)
        if k == 0:
            hidden[...] = term
        else:
            hidden[...] += term

    def finish_last():
        @pl.when(is_end)
        def _():
            p_copy(3, 0).wait_recv()
            base[...] = own[3, z].astype(jnp.float32) + zp[3, z].astype(jnp.float32)

        @pl.when(is_mid)
        def _():
            y_copy(3, 1).wait_recv()
            m_copy(3, 1).wait_recv()
            base[...] = (own[3, z].astype(jnp.float32) + yr[3, z].astype(jnp.float32)) + zm[3, z].astype(jnp.float32)

        for lo in (0, 128):
            rows = slice(lo, lo + 128)

            @pl.when(is_end)
            def _():
                y_tail(lo).wait_recv()
                acc[rows] = (base[rows] + yr[3, z, rows].astype(jnp.float32)).astype(jnp.bfloat16)

            @pl.when(is_mid)
            def _():
                p_tail(lo).wait_recv()
                acc[rows] = (base[rows] + zp[3, z, rows].astype(jnp.float32)).astype(jnp.bfloat16)

            term = jnp.dot(acc[rows], weight_rows(3), preferred_element_type=jnp.float32)
            out_ref[rows] = jnp.maximum(hidden[rows] + term, 0.0).astype(jnp.bfloat16)

    @pl.when(z == 3)
    def _():
        w_up.start()

    @pl.when(is_mid & (y == 1))
    def _():
        w_own_y.start()

    adj[slots] = jnp.zeros((tb, tb), jnp.bfloat16)
    for copy in cp_table:
        copy.wait()
    wide = (128, slots)
    slot = lax.broadcasted_iota(jnp.int32, wide, 1)
    key = jnp.broadcast_to(table[0] * 8 + table[1], wide)
    hit = (key == lax.broadcasted_iota(jnp.int32, wide, 0)) & (slot < count[0, 0])
    found = jnp.min(jnp.where(hit, slot, slots), axis=1, keepdims=True)
    square = (128, 128)
    diagonal = lax.broadcasted_iota(jnp.int32, square, 0) == lax.broadcasted_iota(jnp.int32, square, 1)
    inv_lanes[...] = jnp.min(jnp.where(diagonal, found, slots), axis=0, keepdims=True)
    cp_inv = pltpu.make_async_copy(inv_lanes, inv, lsem.at[5])
    cp_inv.start()

    wait_ready(1)
    f_across.start()
    wait_ready(2)
    f_mate.start()
    wait_ready(3)

    @pl.when(z == 0)
    def _():
        w_up.start()

    cp_inv.wait()
    cp_adj.wait()
    cp_feat.wait()
    mid = 1 - e

    def first(i):
        d = at(i)
        densify(1 - y, d)
        psend[0, d] = product(0, 1 - y, d)
        return i

    def send_first(i):
        @pl.when((i == 3) | (is_end & (i == 2)))
        def _():
            y_copy(0, i).start()

        @pl.when(is_mid & (i == 2))
        def _():
            g_copy(0).start()

        @pl.when(is_end & (i == 0))
        def _():
            b_copy(0).start()

    i_first = first(3 * (y + mid - y * mid))
    wait_ready(0)
    wait_ready(4)

    @pl.when(is_mid & (y == 0))
    def _():
        w_own_y.start()

    send_first(i_first)

    @pl.loop(1, 4)
    def _(step):
        send_first(first(4 - mid - step - 3 * (1 - mid) * y * ((3 - step) // 2)))

    cp_w.wait()

    @pl.when(is_mid)
    def _():
        r_up.wait_recv()
        w_end_y.start()
        w_half_end.start()
        r_own_y.wait_recv()
        w_half.start()
        w_mids.start()

    f_mate.wait_recv()

    @pl.loop(0, 4)
    def _(step):
        i = (3 + e - step) % 4
        d = at(i)
        psend[1, d] = product(1, 1 - y, d)

        @pl.when((i == 3) | (is_end & (i == 2)))
        def _():
            y_copy(1, i).start()

        @pl.when(is_mid & (i == 2))
        def _():
            g_copy(1).start()

        @pl.when(is_end & (i == 0))
        def _():
            b_copy(1).start()

    @pl.when(is_end)
    def _():
        y_copy(0, 1).start()

    def make_own(first, last):
        @pl.loop(first, last)
        def _(step):
            d = at(3 - step)
            densify(y, d)
            own[0, d] = product(0, y, d)
            own[1, d] = product(1, y, d)

    @pl.when(is_end)
    def _():
        make_own(0, 1)
        add_end(0, 3)
        make_own(1, 2)
        add_end(0, 2)
        add_end(1, 3)
        make_own(2, 4)

    @pl.when(is_mid)
    def _():
        merge(0)
        r_half_end.wait_recv()
        w_other_end.start()
        r_half.wait_recv()
        w_other.start()
        merge(1)
        make_own(0, 2)
        r_end_y.wait_recv()
        w_end.start()
        w_half_last.start()
        make_own(2, 4)
        add_mid(0, 3)

    f_across.wait_recv()
    f_fwd.start()

    @pl.loop(0, 4)
    def _(step):
        d = at(3 - step)
        psend[2, d] = product(2, 1 - y, d)

        @pl.when(step == 0)
        def _():
            y_copy(2, 3).start()

    @pl.when(is_end)
    def _():
        add_end(1, 2)

    @pl.when(is_mid)
    def _():
        b_copy(2).start()
        r_half_last.wait_recv()
        w_other_last.start()
        add_mid(0, 2)

    f_fwd.wait_recv()

    @pl.loop(0, 4)
    def _(step):
        d = at(3 - step)
        psend[3, d] = product(3, 1 - y, d)

        @pl.when(step == 0)
        def _():
            y_copy(3, 3).start()

    y_copy(2, 2).start()
    y_copy(3, 2).start()

    @pl.when(is_end)
    def _():
        y_copy(1, 1).start()
        y_copy(2, 1).start()
        y_copy(3, 1).start()
        add_end(0, 1)

    @pl.when(is_mid)
    def _():
        b_copy(3).start()
        v_across.start()
        v_mate.start()

    @pl.loop(0, 4)
    def _(step):
        d = at(3 - step)
        own[2, d] = product(2, y, d)
        own[3, d] = product(3, y, d)

    @pl.when(is_end)
    def _():
        add_end(2, 3)
        add_end(3, 3)
        r_mids.wait_recv()
        r_end.wait_recv()
        r_other.wait_recv()
        r_other_end.wait_recv()
        r_other_last.wait_recv()
        v_across.start()
        v_mate.start()
        merge(2)
        merge_tail()
        add_end(2, 2)
        add_end(3, 2)
        add_end(1, 1)

    @pl.when(is_mid)
    def _():
        add_mid(1, 3)
        gather_mid(0)
        gather_mid(1)
        y_copy(2, 1).start()
        y_copy(3, 1).start()
        add_out(0)
        add_mid(1, 2)
        add_mid(2, 3)
        add_mid(3, 3)
        add_mid(2, 2)

    v_across.wait_recv()
    v_fwd.start()

    @pl.when(is_end)
    def _():
        add_end(2, 1)

    @pl.when(is_mid)
    def _():
        add_out(1)
        add_mid(3, 2)
        add_out(2)

    @pl.when(is_end)
    def _():
        add_end(3, 1)

    @pl.when(is_mid)
    def _():
        add_out(3)

    v_mate.wait_recv()
    v_fwd.wait_recv()
    finish(0)
    finish(1)

    for copy in (f_mate, f_across, f_fwd, v_mate, v_across):
        copy.wait_send()

    @pl.loop(0, 2)
    def _(k):
        y_copy(k, 1).wait_send()
        y_copy(k, 3).wait_send()
        b_copy(k + 2 - 2 * e).wait_send()
        y_copy(k + 2, 3).wait_send()
        y_copy(k + 2, 2).wait_send()

    @pl.when(is_end)
    def _():
        w_up.wait_send()

        @pl.loop(0, 2)
        def _(k):
            y_copy(k, 2).wait_send()
            for i in (1, 2, 3):
                p_copy(k, i).wait_send()
            p_copy(k + 2, 3).wait_send()

    @pl.when(is_mid)
    def _():
        for copy in (w_own_y, w_end_y, w_mids, w_end, w_half, w_half_end, w_half_last, w_other, w_other_end,
                     w_other_last):
            copy.wait_send()

        @pl.loop(0, 2)
        def _(k):
            y_copy(k, 0).wait_send()
            g_copy(k).wait_send()
            p_copy(k, 0).wait_send()
            m_copy(k, 2).wait_send()
            m_copy(k, 3).wait_send()
            m_copy(k + 2, 3).wait_send()

    finish(2)
    finish_last()
    v_fwd.wait_send()
    y_copy(2, 1).wait_send()
    y_copy(3, 1).wait_send()

    @pl.when(is_end)
    def _():
        y_copy(2, 0).wait_send()
        p_copy(2, 2).wait_send()
        p_copy(3, 2).wait_send()
        p_copy(2, 1).wait_send()
        for lo in (0, 128):
            p_tail(lo).wait_send()
            y_tail(lo).wait_send()

    @pl.when(is_mid)
    def _():
        for k in (2, 3):
            m_copy(k, 2).wait_send()
            p_copy(k, 0).wait_send()


def fused_shards(adjacency_tiles, tile_rows, tile_cols, tile_counts, features, weight):
    tiles = adjacency_tiles[0, 0]
    slots, tb = tiles.shape[:2]
    width = features.shape[1]
    wide = weight.shape[1]
    bf = jnp.bfloat16
    dma = pltpu.SemaphoreType.DMA
    blocks = (4, 4, 256, width)
    return pl.pallas_call(
        layer_kernel,
        out_shape=jax.ShapeDtypeStruct((256, wide), bf),
        in_specs=[pl.BlockSpec(memory_space=pltpu.SMEM)]
        + [pl.BlockSpec(memory_space=pltpu.HBM)] * 5,
        out_specs=pl.BlockSpec(memory_space=pltpu.VMEM),
        scratch_shapes=[
            pltpu.VMEM((2, 1, slots), jnp.int32),
            pltpu.VMEM((1, 128), jnp.int32),
            pltpu.SMEM((1, 128), jnp.int32),
            pltpu.VMEM((slots + 1, tb, tb), bf),
            pltpu.VMEM((2, 4, 256, 1024), bf),
            pltpu.VMEM((4, 1024, width), bf),
            pltpu.VMEM((8, 4, weight.shape[0] // 4, wide), bf),
            pltpu.VMEM(blocks, bf),
            pltpu.VMEM(blocks, bf),
            pltpu.VMEM(blocks, bf),
            pltpu.VMEM(blocks, bf),
            pltpu.VMEM(blocks, bf),
            pltpu.VMEM((4, 256, width), bf),
            pltpu.VMEM((2, 256, width), bf),
            pltpu.VMEM((256, width), jnp.float32),
            pltpu.VMEM((256, width), bf),
            pltpu.VMEM((256, wide), jnp.float32),
            dma((6,)),
            dma((3,)), dma((3,)),
            dma((11,)), dma((11,)),
            dma((3,)), dma((3,)),
            dma((4, 4)), dma((4, 4)),
            dma((4, 4)), dma((4, 4)),
            dma((4, 4)), dma((4, 4)),
            dma((4,)), dma((4,)),
            dma((2, 2)),
            dma((4,)), dma((4,)),
            pltpu.SemaphoreType.REGULAR((5,)),
        ],
        compiler_params=pltpu.CompilerParams(
            collective_id=0, has_side_effects=True, vmem_limit_bytes=48 * 2**20),
    )(tile_counts, *(pltpu.with_memory_space_constraint(a, pltpu.HBM)
                     for a in (tile_rows[0], tile_cols[0], tiles, features, weight)))


def solution(mesh):
    fits = mesh.shape["row"] == 4 and mesh.shape["col"] == 8
    return jax.shard_map(
        fused_shards if fits else shards,
        mesh=mesh,
        in_specs=(
            P("row", "col", None, None, None),
            P("row", "col", None),
            P("row", "col", None),
            P("row", "col"),
            P("col", "row"),
            P("col", None),
        ),
        out_specs=P(("row", "col"), None),
        check_vma=False,
    )
```
